256 devices in a mesh: section: 16 (over z_hi, x, core), dp: 16 (over z_lo, y).
Axes of the slice: x: 4, y: 4, z: 8 (z_hi: 2, z_lo: 4; z = z_hi * 4 + z_lo), core: 2. Of those that a mesh axis runs over, the one named last changes fastest.
Arguments:
- examples: bfloat16 [2, 2048, 2048], P(None, 'dp'), may hold values from -6 to 6
- arriving: float32 [16, 2048, 2048], P('section', 'dp'), may hold values from -6 to 6
- returning: float32 [16, 2048, 2048], P('section', 'dp'), may hold values from -6 to 6
- stash: bfloat16 [16, 2, 2048, 2048], P('section', None, 'dp'), may hold values from -6 to 6
- plan: int32 [16, 2], P('section'), may hold values from 0 to 1, each once within a row
- forward_expert_routes: int32 [16, 2, 2048, 8], P('section', None, 'dp'), may hold values from 0 to 127, as said below
- backward_expert_routes: int32 [16, 2, 2048, 8], P('section', None, 'dp'), may hold values from 0 to 127, as said below
- input_norm_gain: float32 [16, 2048], P('section'), may hold values from 0.1 to 1.9
- router: bfloat16 [16, 2048, 128], P('section'), may hold values from -0.125 to 0.125
- frozen_gate_weight: bfloat16 [16, 2048, 384], P('section'), may hold values from -0.125 to 0.125
- frozen_up_weight: bfloat16 [16, 2048, 384], P('section'), may hold values from -0.125 to 0.125
- frozen_down_weight: bfloat16 [16, 384, 2048], P('section'), may hold values from -0.3125 to 0.3125
- down_factors: bfloat16 [16, 2048, 64], P('section'), may hold values from -0.125 to 0.125
- up_factors: bfloat16 [16, 2, 32, 384], P('section'), may hold values from -0.5 to 0.5
Outputs:
- next_acts: float32 [16, 2048, 2048], P('section', 'dp')
- next_grads: float32 [16, 2048, 2048], P('section', 'dp')
- grad_a: float32 [16, 2048, 64], P('section', 'dp')
- grad_b: float32 [16, 2, 32, 384], P('section', None, None, 'dp')
The draws below stay inside these ranges and needn't reach their ends.
Inputs may be any that keep to these rules, and one draw needn't show every extreme that they name: forward_expert_routes[..., 0] is 0 for every token: each section holds expert 0 of its layer. The other 7 entries of a token are distinct numbers from 1 to 127. `backward_expert_routes`: as forward_expert_routes: entry 0 is 0, the rest distinct from 1 to 127. `plan`: each section's row is a permutation of 0 to 1.
All inputs are finite; a program needn't handle non-finite values.
Results may differ from the reference program's by a relative error of at most 0.015.
Values sent between devices are 32-bit elements; how exact they have to be, the bound alone decides.
No kernel may reach another device: no remote copies, remote signals or barrier semaphores. Data moves between devices by JAX's collectives and lax.ppermute only.
A program may use at most 64 MiB of HBM per device.

```python
import jax
import jax.numpy as jnp
from jax import lax

MODEL_WIDTH = 2048
HIDDEN_UNITS = 384
EXPERTS = 128
TOPK = 8
ADAPTER_RANK = 32
TICKS = 2
TOK = 128
RELAY_SECTIONS = 16
TOKENS = 2048
N_DP = 16


def routes_common(key):
    row_count = RELAY_SECTIONS * TICKS * TOKENS
    keys = jax.random.split(key, row_count)

    def pick_row(row_key):
        return jax.random.permutation(row_key, EXPERTS - 1)[:TOPK - 1] + 1
    others = jax.vmap(pick_row)(keys).astype(jnp.int32)
    leading = jnp.zeros((row_count, 1), jnp.int32)
    return jnp.concatenate([leading, others], axis=1).reshape(RELAY_SECTIONS, TICKS, TOKENS, TOPK)


def draw_forward_expert_routes(key, part):
    return routes_common(jax.random.fold_in(key, 11))


def draw_backward_expert_routes(key, part):
    return routes_common(jax.random.fold_in(key, 23))


def block_scale(stream_key, shape, cuts, low, high):
    gain = 1.0
    for dim, parts in cuts:
        heights = jax.random.uniform(jax.random.fold_in(jax.random.fold_in(stream_key, 6), dim), (parts,), jnp.float32, low / len(cuts), high / len(cuts))
        gain = gain * jnp.repeat(jnp.exp(heights), shape[dim] // parts).reshape((-1,) + (1,) * (len(shape) - 1 - dim))
    return gain


def gaussian(key, extent, scale, limit, pieces=(), held_as=jnp.bfloat16):
    gain = block_scale(key, extent, pieces, -0.22, 0.18) if pieces else 1.0
    drawn = jax.random.normal(key, extent, jnp.float32) * scale * gain
    return jnp.minimum(jnp.maximum(drawn, -limit), limit).astype(held_as)


def setup_inputs(seed: int = 0) -> dict:
    splits = jax.random.split(jax.random.key(seed), 15)
    return {
        "examples": gaussian(splits[0], (TICKS, TOKENS, MODEL_WIDTH), 1.0, 6.0, ((1, 16),)),
        "arriving": gaussian(splits[1], (RELAY_SECTIONS, TOKENS, MODEL_WIDTH), 1.0, 6.0, ((0, 16), (1, 16)), jnp.float32),
        "returning": gaussian(splits[2], (RELAY_SECTIONS, TOKENS, MODEL_WIDTH), 1.0, 6.0, ((0, 16), (1, 16)), jnp.float32),
        "stash": gaussian(splits[3], (RELAY_SECTIONS, TICKS, TOKENS, MODEL_WIDTH), 1.0, 6.0, ((0, 16), (2, 16))),
        "plan": jax.vmap(lambda own: jax.random.permutation(own, TICKS))(jax.random.split(splits[4], RELAY_SECTIONS)).reshape((RELAY_SECTIONS, TICKS)).astype(jnp.int32),
        "forward_expert_routes": draw_forward_expert_routes(jax.random.fold_in(splits[14], 71), 0),
        "backward_expert_routes": draw_backward_expert_routes(jax.random.fold_in(splits[14], 71), 0),
        "input_norm_gain": jnp.clip(1.0 + 0.18 * jax.random.normal(splits[7], (RELAY_SECTIONS, MODEL_WIDTH), jnp.float32), 0.1, 1.9),
        "router": gaussian(splits[8], (RELAY_SECTIONS, MODEL_WIDTH, EXPERTS), MODEL_WIDTH ** -0.5, 0.125, ((0, 16),)),
        "frozen_gate_weight": gaussian(splits[9], (RELAY_SECTIONS, MODEL_WIDTH, HIDDEN_UNITS), MODEL_WIDTH ** -0.5, 0.125, ((0, 16),)),
        "frozen_up_weight": gaussian(splits[10], (RELAY_SECTIONS, MODEL_WIDTH, HIDDEN_UNITS), MODEL_WIDTH ** -0.5, 0.125, ((0, 16),)),
        "frozen_down_weight": gaussian(splits[11], (RELAY_SECTIONS, HIDDEN_UNITS, MODEL_WIDTH), HIDDEN_UNITS ** -0.5, 0.3125, ((0, 16),)),
        "down_factors": gaussian(splits[12], (RELAY_SECTIONS, MODEL_WIDTH, 2 * ADAPTER_RANK), MODEL_WIDTH ** -0.5, 0.125, ((0, 16),)),
        "up_factors": gaussian(splits[13], (RELAY_SECTIONS, 2, ADAPTER_RANK, HIDDEN_UNITS), (4 * ADAPTER_RANK) ** -0.5, 0.5, ((0, 16),)),
    }


adapter_scale = 2.0

def apply_layer(inputs, routes, frozen, adapter_down, adapter_up):
    gain_vec, router_w, gate_matrix, up_matrix, down_w = frozen
    inputs_f = inputs.astype(jnp.float32)
    mean_square = lax.optimization_barrier(jnp.mean(inputs_f * inputs_f, axis=-1, keepdims=True))
    normalized_input = (inputs_f * lax.rsqrt(mean_square + 1e-06) * gain_vec).astype(jnp.bfloat16)
    logits = jnp.dot(normalized_input, router_w, preferred_element_type=jnp.float32)
    one_hot = (routes[:, :, None] == jnp.arange(router_w.shape[1], dtype=jnp.int32)[None, None, :]).astype(jnp.float32)
    picked = jnp.einsum('tke,te->tk', one_hot, logits.astype(jnp.float32))
    scores = jnp.exp(picked)
    weight = scores[:, 0] / lax.optimization_barrier(jnp.sum(scores, axis=-1))
    factor_rank = adapter_down.shape[1] // 2
    reduced_rank_output = jnp.dot(normalized_input, adapter_down.astype(jnp.bfloat16), preferred_element_type=jnp.float32).astype(jnp.bfloat16)
    up_factor_matrix = adapter_up.astype(jnp.bfloat16)
    gate_preactivation = jnp.dot(normalized_input, gate_matrix, preferred_element_type=jnp.float32) + adapter_scale * jnp.dot(reduced_rank_output[:, :factor_rank], up_factor_matrix[0], preferred_element_type=jnp.float32)
    up_preactivation = jnp.dot(normalized_input, up_matrix, preferred_element_type=jnp.float32) + adapter_scale * jnp.dot(reduced_rank_output[:, factor_rank:], up_factor_matrix[1], preferred_element_type=jnp.float32)
    hidden = (jax.nn.silu(gate_preactivation) * up_preactivation).astype(jnp.bfloat16)
    branch = jnp.dot(hidden, down_w, preferred_element_type=jnp.float32)
    return inputs_f + weight[:, None] * branch

def normalizer(grad_a, grad_b):
    entries = grad_a.size + grad_b.size
    mean_square = (jnp.sum(grad_a * grad_a) + jnp.sum(grad_b * grad_b)) / entries
    return lax.rsqrt(mean_square + 1e-06)

def example_step(inputs, routes, cotangent, frozen, adapter_down, adapter_up):

    def closed(values, first_a, first_b):
        return apply_layer(values, routes, frozen, first_a, first_b)
    result, pullback = jax.vjp(closed, inputs, adapter_down, adapter_up)
    d_input, grad_a, grad_b = pullback(cotangent)
    factor = normalizer(grad_a, grad_b)
    return (d_input, factor * grad_a, factor * grad_b)

def reference(examples, arriving, returning, stash, plan, forward_expert_routes, backward_expert_routes, input_norm_gain, router, frozen_gate_weight, frozen_up_weight, frozen_down_weight, down_factors, up_factors):
    ex_blocks = examples.reshape(TICKS, N_DP, TOK, MODEL_WIDTH).astype(jnp.float32)
    fwd_in = arriving.reshape(RELAY_SECTIONS, N_DP, TOK, MODEL_WIDTH)
    back_in = returning.reshape(RELAY_SECTIONS, N_DP, TOK, MODEL_WIDTH)
    stash_blocks = stash.reshape(RELAY_SECTIONS, TICKS, N_DP, TOK, MODEL_WIDTH)
    fwd_routes = forward_expert_routes.reshape(RELAY_SECTIONS, TICKS, N_DP, TOK, TOPK)
    bwd_routes = backward_expert_routes.reshape(RELAY_SECTIONS, TICKS, N_DP, TOK, TOPK)
    frozen = (input_norm_gain, router, frozen_gate_weight, frozen_up_weight, frozen_down_weight)
    adapter_down = down_factors.astype(jnp.float32)
    adapter_up = up_factors.astype(jnp.float32)
    section_ids = jnp.arange(RELAY_SECTIONS, dtype=jnp.int32)
    first_mask = (section_ids == 0)[:, None, None, None]
    last_mask = (section_ids == RELAY_SECTIONS - 1)[:, None, None, None]
    forward_all = jax.vmap(jax.vmap(apply_layer, in_axes=(0, 0, None, None, None)))
    backward_all = jax.vmap(jax.vmap(example_step, in_axes=(0, 0, 0, None, None, None)))
    total_a = jnp.zeros(adapter_down.shape, jnp.float32)
    total_b = jnp.zeros(adapter_up.shape, jnp.float32)
    for tick_index in range(TICKS):
        source = jnp.where(first_mask, ex_blocks[tick_index][None], fwd_in)
        routes_now = fwd_routes[:, tick_index]
        output = forward_all(source, routes_now, frozen, adapter_down, adapter_up)
        slot_index = plan[:, tick_index].astype(jnp.int32)
        stashed = stash_blocks[section_ids, slot_index].astype(jnp.float32)
        stashed_routes = bwd_routes[section_ids, slot_index]
        primal_in = jnp.where(last_mask, source, stashed)
        primal_routes = jnp.where(last_mask, routes_now, stashed_routes)
        loss_grad = output - ex_blocks[tick_index][None]
        incoming = jnp.where(last_mask, loss_grad, back_in)
        d_input, share_a, share_b = backward_all(primal_in, primal_routes, incoming, frozen, adapter_down, adapter_up)
        total_a = total_a + lax.optimization_barrier(jnp.sum(share_a, axis=1))
        total_b = total_b + lax.optimization_barrier(jnp.sum(share_b, axis=1))
        fwd_in = jnp.concatenate([jnp.zeros_like(output[:1]), output[:-1]], axis=0)
        back_in = jnp.concatenate([d_input[1:], jnp.zeros_like(d_input[:1])], axis=0)
    divisor = TICKS * N_DP
    return (fwd_in.reshape(RELAY_SECTIONS, TOKENS, MODEL_WIDTH), back_in.reshape(RELAY_SECTIONS, TOKENS, MODEL_WIDTH), total_a / divisor, total_b / divisor)
```

```python
import functools

import jax
import jax.numpy as jnp
from jax import lax
from jax.experimental import pallas as pl
from jax.experimental.pallas import tpu as pltpu
from jax.sharding import PartitionSpec as P

SCALE = 2.0
EPS = 1e-06
F32 = jnp.float32
BF16 = jnp.bfloat16
ANY = pl.BlockSpec(memory_space=pl.ANY)
SMEM = pl.BlockSpec(memory_space=pltpu.SMEM)
VMEM = pl.BlockSpec(memory_space=pltpu.VMEM)


def nn(a, b):
    return jnp.dot(a, b, preferred_element_type=F32)


def nt(a, b):
    return lax.dot_general(a, b, (((1,), (1,)), ((), ())), preferred_element_type=F32)


class Loads:
    def __init__(self, sems):
        self.sems = sems
        self.used = 0

    def start(self, source, target):
        copy = pltpu.make_async_copy(source, target, self.sems.at[self.used])
        self.used += 1
        copy.start()
        return copy


def primal(x, routes_t, gain, copies, router, a_t, gate, up, factors):
    rstd = lax.rsqrt(jnp.mean(x * x, axis=-1, keepdims=True) + EPS)
    normed = (x * rstd * gain).astype(BF16)
    copies["router"].wait()
    logits = nn(normed, router[...])
    experts = logits.shape[1]
    expert = lax.broadcasted_iota(jnp.int32, (experts, routes_t.shape[1]), 0)
    named = jnp.zeros(expert.shape, F32)
    for k in range(routes_t.shape[0]):
        named = jnp.where(routes_t[k : k + 1, :] == expert, 1.0, named)
    scores = jnp.where(named.T > 0.5, jnp.exp(logits), 0.0)
    share = scores / jnp.sum(scores, axis=-1, keepdims=True)
    weight = share[:, 0:1]
    copies["a"].wait()
    low = nt(normed, a_t[...]).astype(BF16)
    rank = low.shape[1] // 2
    copies["b"].wait()
    copies["gate"].wait()
    gate_pre = nn(normed, gate[...]) + SCALE * nn(low[:, :rank], factors[0])
    copies["up"].wait()
    up_pre = nn(normed, up[...]) + SCALE * nn(low[:, rank:], factors[1])
    return rstd, normed, share, weight, low, gate_pre, up_pre


def forward_kernel(
    tick,
    arriving,
    examples,
    routes_t,
    gain,
    router_h,
    a_h,
    gate_h,
    up_h,
    b_h,
    down_h,
    out,
    x_s,
    ex_s,
    r_s,
    gain_s,
    router,
    a_t,
    gate,
    up,
    factors,
    down,
    sems,
):
    first = lax.axis_index("section") == 0
    loads = Loads(sems)
    x_copy = pltpu.make_async_copy(arriving, x_s, sems.at[0])
    ex_copy = pltpu.make_async_copy(examples.at[tick], ex_s, sems.at[1])
    loads.used = 2

    @pl.when(first)
    def _():
        ex_copy.start()

    @pl.when(jnp.logical_not(first))
    def _():
        x_copy.start()

    copies = {}
    copies["gain"] = loads.start(gain, gain_s)
    copies["routes"] = loads.start(routes_t.at[tick], r_s)
    copies["router"] = loads.start(router_h, router)
    copies["a"] = loads.start(a_h, a_t)
    copies["b"] = loads.start(b_h, factors)
    copies["gate"] = loads.start(gate_h, gate)
    copies["up"] = loads.start(up_h, up)
    copies["down"] = loads.start(down_h, down)

    @pl.when(first)
    def _():
        ex_copy.wait()
        x_s[...] = ex_s[...].astype(F32)

    @pl.when(jnp.logical_not(first))
    def _():
        x_copy.wait()

    copies["gain"].wait()
    copies["routes"].wait()
    x = x_s[...]
    _, _, _, weight, _, gate_pre, up_pre = primal(
        x, r_s[...], gain_s[...], copies, router, a_t, gate, up, factors
    )
    hidden = (gate_pre * jax.nn.sigmoid(gate_pre) * up_pre).astype(BF16)
    copies["down"].wait()
    out[...] = x_s[...] + weight * nn(hidden, down[...])


def backward_kernel(
    tick,
    last_tick,
    mean_scale,
    plan,
    arriving,
    returning,
    examples,
    stash,
    fwd_routes_t,
    bwd_routes_t,
    gain,
    router_h,
    a_h,
    gate_h,
    up_h,
    b_h,
    down_h,
    *rest,
):
    if last_tick:
        ga_in, gb_in, dx, packed = rest[:4]
        rest = rest[4:]
    else:
        dx, ga_out, gb_out = rest[:3]
        rest = rest[3:]
    x_s, g_s, ex_s, st_s, r_s, gain_s, router, a_t, gate, up, factors, down, sems = rest
    last = lax.axis_index("section") == lax.axis_size("section") - 1
    other = jnp.logical_not(last)
    slot = plan[0, tick]
    loads = Loads(sems)
    loads.used = 6
    x_copy = pltpu.make_async_copy(arriving, x_s, sems.at[0])
    ex_copy = pltpu.make_async_copy(examples.at[tick], ex_s, sems.at[1])
    fr_copy = pltpu.make_async_copy(fwd_routes_t.at[tick], r_s, sems.at[2])
    st_copy = pltpu.make_async_copy(stash.at[slot], st_s, sems.at[3])
    g_copy = pltpu.make_async_copy(returning, g_s, sems.at[4])
    br_copy = pltpu.make_async_copy(bwd_routes_t.at[slot], r_s, sems.at[5])

    @pl.when(last)
    def _():
        x_copy.start()
        fr_copy.start()
        ex_copy.start()

    @pl.when(other)
    def _():
        st_copy.start()
        br_copy.start()

    copies = {}
    copies["gain"] = loads.start(gain, gain_s)
    copies["router"] = loads.start(router_h, router)
    copies["a"] = loads.start(a_h, a_t)
    copies["b"] = loads.start(b_h, factors)
    copies["gate"] = loads.start(gate_h, gate)
    copies["up"] = loads.start(up_h, up)
    copies["down"] = loads.start(down_h, down)

    @pl.when(other)
    def _():
        g_copy.start()
        st_copy.wait()
        br_copy.wait()
        x_s[...] = st_s[...].astype(F32)

    @pl.when(last)
    def _():
        x_copy.wait()
        fr_copy.wait()

    copies["gain"].wait()
    rstd, normed, share, weight, low, gate_pre, up_pre = primal(
        x_s[...], r_s[...], gain_s[...], copies, router, a_t, gate, up, factors
    )
    sig = jax.nn.sigmoid(gate_pre)
    silu = gate_pre * sig
    hidden = (silu * up_pre).astype(BF16)
    copies["down"].wait()

    @pl.when(last)
    def _():
        ex_copy.wait()
        g_s[...] = x_s[...] + weight * nn(hidden, down[...]) - ex_s[...].astype(F32)

    @pl.when(other)
    def _():
        g_copy.wait()

    back = nt(g_s[...].astype(BF16), down[...])
    d_weight = jnp.sum(hidden.astype(F32) * back, axis=-1, keepdims=True)
    lead = (lax.broadcasted_iota(jnp.int32, share.shape, 1) == 0).astype(F32)
    d_logits = ((d_weight * weight) * (lead - share)).astype(BF16)
    d_hidden = (weight * back).astype(BF16).astype(F32)
    d_gate = (d_hidden * up_pre * (sig * (1.0 + gate_pre * (1.0 - sig)))).astype(BF16)
    d_up = (d_hidden * silu).astype(BF16)
    d_low_f = SCALE * jnp.concatenate([nt(d_gate, factors[0]), nt(d_up, factors[1])], axis=1)
    d_low = d_low_f.astype(BF16)
    d_normed = (
        nt(d_logits, router[...])
        + nn(d_low, a_t[...])
        + nt(d_gate, gate[...])
        + nt(d_up, up[...])
    )
    scaled = d_normed * gain_s[...]
    x = x_s[...]
    along = jnp.mean(scaled * x, axis=-1, keepdims=True) * (rstd * rstd)
    dx[...] = g_s[...] + rstd * (scaled - x * along)

    rank = low.shape[1] // 2
    ga = nn(d_low_f.T.astype(BF16), normed)
    low_t = low.astype(F32).T.astype(BF16)
    gb = SCALE * jnp.concatenate([nn(low_t[:rank], d_gate), nn(low_t[rank:], d_up)], axis=0)
    entries = ga.size + gb.size
    square = (jnp.sum(ga * ga) + jnp.sum(gb * gb)) / entries
    factor = lax.rsqrt(square + EPS) * mean_scale
    if not last_tick:
        ga_out[...] = factor * ga
        gb_out[...] = factor * gb
        return
    ga = ga_in[...] + factor * ga
    gb_t = (gb_in[...] + factor * gb).T
    ys, zs = packed.shape[:2]
    width = ga.shape[1] // (ys * zs)
    rows = gb_t.shape[0] // (ys * zs)
    tall = ga.shape[0]
    half = rows // 2
    for y in range(ys):
        for z in range(zs):
            p = z * ys + y
            packed[y, z, :tall, :] = ga[:, p * width : (p + 1) * width]
            packed[y, z, tall : tall + half, :tall] = gb_t[p * rows : p * rows + half]
            packed[y, z, tall : tall + half, tall:] = gb_t[p * rows + half : (p + 1) * rows]
            packed[y, z, tall + half :, :] = jnp.zeros((packed.shape[2] - tall - half, width), F32)


def sum_kernel(parts, total):
    total[...] = jnp.sum(parts[...], axis=0)


def final_kernel(tall, half, parts, ga, gb):
    total = jnp.sum(parts[...], axis=0)
    ga[...] = total[:tall]
    rank = gb.shape[2]
    for side in range(2):
        for part in range(2):
            lane = part * tall + side * rank
            gb[side, part * half : (part + 1) * half, :] = total[
                tall : tall + half, lane : lane + rank
            ]


def shifted(value, axis, steps):
    count = lax.axis_size(axis)
    initial, last = (max(0, -steps), min(count, count - steps))
    return lax.ppermute(value, axis, [(source, source + steps) for source in range(initial, last)])


def shards(
    y_size,
    examples,
    arriving,
    returning,
    stash,
    plan,
    forward_expert_routes,
    backward_expert_routes,
    input_norm_gain,
    router,
    frozen_gate_weight,
    frozen_up_weight,
    frozen_down_weight,
    down_factors,
    up_factors,
):
    replicas = lax.axis_size("dp")
    z_size = replicas // y_size
    ticks, tokens, width = examples.shape
    mean_scale = 1.0 / (ticks * replicas)
    gain, router, gate, up, down = (
        input_norm_gain,
        router[0],
        frozen_gate_weight[0],
        frozen_up_weight[0],
        frozen_down_weight[0],
    )
    a_t = down_factors[0].T
    b = up_factors[0]
    stash = stash[0]
    fwd_routes_t = jnp.swapaxes(forward_expert_routes[0], 1, 2)
    bwd_routes_t = jnp.swapaxes(backward_expert_routes[0], 1, 2)
    topk = fwd_routes_t.shape[1]
    hidden_units = gate.shape[1]
    columns = a_t.shape[0]
    weights = (gain, router, a_t, gate, up, b, down)
    weight_scratch = [pltpu.VMEM(w.shape, w.dtype) for w in weights]
    activation = jax.ShapeDtypeStruct((tokens, width), F32)
    params = pltpu.CompilerParams(vmem_limit_bytes=40 << 20)
    primal_flops = 2 * tokens * width * (router.shape[1] + columns + 2 * hidden_units)
    down_flops = 2 * tokens * width * hidden_units
    weight_bytes = sum(w.size * w.dtype.itemsize for w in weights)

    def forward(tick, source):
        return pl.pallas_call(
            functools.partial(forward_kernel, tick),
            out_shape=activation,
            in_specs=[ANY] * (3 + len(weights)),
            out_specs=VMEM,
            scratch_shapes=[
                pltpu.VMEM((tokens, width), F32),
                pltpu.VMEM((tokens, width), BF16),
                pltpu.VMEM((topk, tokens), jnp.int32),
                *weight_scratch,
                pltpu.SemaphoreType.DMA((10,)),
            ],
            compiler_params=params,
            cost_estimate=pl.CostEstimate(
                flops=primal_flops + down_flops,
                bytes_accessed=weight_bytes + 8 * tokens * width,
                transcendentals=0,
            ),
            name="forward_%d" % tick,
        )(source, examples, fwd_routes_t, *weights)

    gb_rows = columns
    rows_each = hidden_units // replicas
    packed_rows = columns + -(-(rows_each // 2) // 8) * 8

    def backward(tick, source, returned, sums):
        last_tick = tick == ticks - 1
        if last_tick:
            outs = (
                activation,
                jax.ShapeDtypeStruct((y_size, z_size, packed_rows, width // replicas), F32),
            )
        else:
            outs = (
                activation,
                jax.ShapeDtypeStruct((columns, width), F32),
                jax.ShapeDtypeStruct((gb_rows, hidden_units), F32),
            )
        return pl.pallas_call(
            functools.partial(backward_kernel, tick, last_tick, mean_scale),
            out_shape=outs,
            in_specs=[SMEM] + [ANY] * (6 + len(weights)) + [VMEM] * len(sums),
            out_specs=tuple(VMEM for _ in outs),
            scratch_shapes=[
                pltpu.VMEM((tokens, width), F32),
                pltpu.VMEM((tokens, width), F32),
                pltpu.VMEM((tokens, width), BF16),
                pltpu.VMEM((tokens, width), BF16),
                pltpu.VMEM((topk, tokens), jnp.int32),
                *weight_scratch,
                pltpu.SemaphoreType.DMA((13,)),
            ],
            compiler_params=params,
            cost_estimate=pl.CostEstimate(
                flops=2 * primal_flops + down_flops,
                bytes_accessed=weight_bytes + 10 * tokens * width,
                transcendentals=0,
            ),
            name="backward_%d" % tick,
        )(plan, source, returned, examples, stash, fwd_routes_t, bwd_routes_t, *weights, *sums)

    forward_in = arriving[0]
    backward_in = returning[0]
    sums = ()
    for tick in range(ticks):
        output = forward(tick, forward_in)
        source = forward_in
        forward_in = shifted(output, "section", 1)
        d_input, *sums = backward(tick, source, backward_in, sums)
        backward_in = shifted(d_input, "section", -1)
    packed = sums[0]
    y_groups = [[z * y_size + y for y in range(y_size)] for z in range(z_size)]
    z_groups = [[z * y_size + y for z in range(z_size)] for y in range(y_size)]
    parts = lax.all_to_all(packed, "dp", 0, 0, axis_index_groups=y_groups, tiled=True)
    parts = pl.pallas_call(
        sum_kernel,
        out_shape=jax.ShapeDtypeStruct(parts.shape[1:], F32),
        in_specs=[VMEM],
        out_specs=VMEM,
        name="sum_y",
    )(parts)
    parts = lax.all_to_all(parts, "dp", 0, 0, axis_index_groups=z_groups, tiled=True)
    share_a, share_b = pl.pallas_call(
        functools.partial(final_kernel, columns, rows_each // 2),
        out_shape=(
            jax.ShapeDtypeStruct((columns, width // replicas), F32),
            jax.ShapeDtypeStruct((2, rows_each, columns // 2), F32),
        ),
        in_specs=[VMEM],
        out_specs=(VMEM, VMEM),
        name="sum_z",
    )(parts)
    return (
        forward_in[None],
        backward_in[None],
        share_a.T[None],
        jnp.swapaxes(share_b, 1, 2)[None],
    )


def solution(mesh):
    in_specs = (
        P(None, "dp", None),
        P("section", "dp", None),
        P("section", "dp", None),
        P("section", None, "dp", None),
        P("section", None),
        P("section", None, "dp", None),
        P("section", None, "dp", None),
        P("section", None),
        P("section", None, None),
        P("section", None, None),
        P("section", None, None),
        P("section", None, None),
        P("section", None, None),
        P("section", None, None, None),
    )
    out_specs = (
        P("section", "dp", None),
        P("section", "dp", None),
        P("section", "dp", None),
        P("section", None, None, "dp"),
    )
    return jax.shard_map(
        functools.partial(shards, 4),
        mesh=mesh,
        in_specs=in_specs,
        out_specs=out_specs,
        check_vma=False,
    )
```

```python
import functools

import jax
import jax.numpy as jnp
from jax import lax
from jax.experimental import pallas as pl
from jax.experimental.pallas import tpu as pltpu
from jax.sharding import PartitionSpec as P


SCALE = 2.0
EPS = 1e-06
F32 = jnp.float32
BF16 = jnp.bfloat16
ANY = pl.BlockSpec(memory_space=pl.ANY)
SMEM = pl.BlockSpec(memory_space=pltpu.SMEM)
VMEM = pl.BlockSpec(memory_space=pltpu.VMEM)


def nn(a, b):
    return jnp.dot(a, b, preferred_element_type=F32)


def nt(a, b):
    return lax.dot_general(a, b, (((1,), (1,)), ((), ())), preferred_element_type=F32)


def primal(x, routes_t, gain, copies, router, a_t, gate, up, factors):
    rstd = lax.rsqrt(jnp.mean(x * x, axis=-1, keepdims=True) + EPS)
    normed = (x * rstd * gain).astype(BF16)
    copies["router"].wait()
    logits = nn(normed, router[...])
    experts = logits.shape[1]
    expert = lax.broadcasted_iota(jnp.int32, (experts, routes_t.shape[1]), 0)
    named = jnp.zeros(expert.shape, F32)
    for k in range(routes_t.shape[0]):
        named = jnp.where(routes_t[k : k + 1, :] == expert, 1.0, named)
    scores = jnp.where(named.T > 0.5, jnp.exp(logits), 0.0)
    share = scores / jnp.sum(scores, axis=-1, keepdims=True)
    weight = share[:, 0:1]
    copies["a"].wait()
    low = nt(normed, a_t[...]).astype(BF16)
    rank = low.shape[1] // 2
    copies["b"].wait()
    copies["gate"].wait()
    gate_pre = nn(normed, gate[...]) + SCALE * nn(low[:, :rank], factors[0])
    copies["up"].wait()
    up_pre = nn(normed, up[...]) + SCALE * nn(low[:, rank:], factors[1])
    return rstd, normed, share, weight, low, gate_pre, up_pre


def when_all(*predicates):
    both = predicates[0]
    for predicate in predicates[1:]:
        both = jnp.logical_and(both, predicate)
    return pl.when(both)


def position():
    section = lax.axis_index("section")
    odd = lax.rem(section, 2) == 1
    return (
        odd,
        jnp.logical_not(odd),
        section == 0,
        section == lax.axis_size("section") - 1,
    )


def fetch(cases, x_s, b_s, r_s, sems):
    moves = []
    for predicates, source, routes in cases:
        narrow = source.dtype == BF16
        x_copy = pltpu.make_async_copy(source, b_s if narrow else x_s, sems.at[0])
        r_copy = pltpu.make_async_copy(routes, r_s, sems.at[1])
        moves.append((predicates, narrow, x_copy, r_copy))

        @when_all(*predicates)
        def _(x_copy=x_copy, r_copy=r_copy):
            x_copy.start()
            r_copy.start()

    def wait():
        for predicates, narrow, x_copy, r_copy in moves:

            @when_all(*predicates)
            def _(narrow=narrow, x_copy=x_copy, r_copy=r_copy):
                x_copy.wait()
                r_copy.wait()
                if narrow:
                    x_s[...] = b_s[...].astype(F32)

    return wait


def fetch_cotangent(cases, g_s, e_s, sems):
    moves = []
    for predicates, source, target in cases:
        g_copy = pltpu.make_async_copy(source, g_s, sems.at[2])
        t_copy = None if target is None else pltpu.make_async_copy(target, e_s, sems.at[3])
        moves.append((predicates, g_copy, t_copy))

        @when_all(*predicates)
        def _(g_copy=g_copy, t_copy=t_copy):
            g_copy.start()
            if t_copy is not None:
                t_copy.start()

    def wait():
        for predicates, g_copy, t_copy in moves:

            @when_all(*predicates)
            def _(g_copy=g_copy, t_copy=t_copy):
                g_copy.wait()
                if t_copy is not None:
                    t_copy.wait()
                    g_s[...] = g_s[...] - e_s[...].astype(F32)

    return wait


NAMES = ("gain", "router", "a", "gate", "up", "b", "down")


def fetch_weights(hbm, weights, order, sems):
    copies = {}
    for name in order:
        i = NAMES.index(name)
        copies[name] = pltpu.make_async_copy(hbm[i], weights[i], sems.at[4 + i])
        copies[name].start()
    return copies


def primal_of(x, routes, copies, weights):
    gain_s, router, a_t, gate, up, factors = weights[:6]
    copies["gain"].wait()
    return primal(x, routes, gain_s[...], copies, router, a_t, gate, up, factors)


def output_of(x_s, values, down):
    _, _, _, weight, _, gate_pre, up_pre = values
    hidden = (gate_pre * jax.nn.sigmoid(gate_pre) * up_pre).astype(BF16)
    return x_s[...] + weight * nn(hidden, down[...])


def gradients(x_s, g_s, saved, weights):
    gain_s, router, a_t, gate, up, factors, down = weights
    rstd, normed, share, weight, low, gate_pre, up_pre = saved
    sig = jax.nn.sigmoid(gate_pre)
    silu = gate_pre * sig
    hidden = (silu * up_pre).astype(BF16)
    back = nt(g_s[...].astype(BF16), down[...])
    d_weight = jnp.sum(hidden.astype(F32) * back, axis=-1, keepdims=True)
    lead = (lax.broadcasted_iota(jnp.int32, share.shape, 1) == 0).astype(F32)
    d_logits = ((d_weight * weight) * (lead - share)).astype(BF16)
    d_hidden = (weight * back).astype(BF16).astype(F32)
    d_gate = (d_hidden * up_pre * (sig * (1.0 + gate_pre * (1.0 - sig)))).astype(BF16)
    d_up = (d_hidden * silu).astype(BF16)
    d_low_f = SCALE * jnp.concatenate([nt(d_gate, factors[0]), nt(d_up, factors[1])], axis=1)
    d_normed = (
        nt(d_gate, gate[...])
        + nt(d_up, up[...])
        + nt(d_logits, router[...])
        + nn(d_low_f.astype(BF16), a_t[...])
    )
    scaled = d_normed * gain_s[...]
    x = x_s[...]
    along = jnp.mean(scaled * x, axis=-1, keepdims=True) * (rstd * rstd)
    dx = g_s[...] + rstd * (scaled - x * along)
    rank = low.shape[1] // 2
    ga = nn(d_low_f.T.astype(BF16), normed)
    low_t = low.astype(F32).T.astype(BF16)
    gb = SCALE * jnp.concatenate([nn(low_t[:rank], d_gate), nn(low_t[rank:], d_up)], axis=0)
    return dx, ga, gb


def normalizer(ga, gb, mean_scale):
    square = (jnp.sum(ga * ga) + jnp.sum(gb * gb)) / (ga.size + gb.size)
    return lax.rsqrt(square + EPS) * mean_scale


def pack(packed, ga, gb):
    gb_t = gb.T
    ys = packed.shape[0]
    width = packed.shape[2]
    zs = ga.shape[1] // (ys * width)
    size = packed.shape[1] // zs
    rows = gb_t.shape[0] // (ys * zs)
    tall = ga.shape[0]
    half = rows // 2
    for y in range(ys):
        for z in range(zs):
            p = z * ys + y
            at = z * size
            packed[y, at : at + tall, :] = ga[:, p * width : (p + 1) * width]
            packed[y, at + tall : at + tall + half, :tall] = gb_t[p * rows : p * rows + half]
            packed[y, at + tall : at + tall + half, tall:] = gb_t[p * rows + half : (p + 1) * rows]
            packed[y, at + tall + half : at + size, :] = jnp.zeros((size - tall - half, width), F32)


FIRST_ORDER = ("gain", "router", "a", "b", "gate", "up", "down")


def step_kernel(
    tick,
    odd_forward,
    mean_scale,
    plan,
    act_in,
    grad_in,
    output,
    examples,
    stash,
    fwd_routes_t,
    bwd_routes_t,
    *rest,
):
    hbm, rest = rest[:7], rest[7:]
    if tick:
        ga_in, gb_in, sent, packed, *rest = rest
    else:
        sent, ga_out, gb_out, *rest = rest
    x_s, g_s, b_s, e_s, r_s, *weights, sems = rest
    odd, even, first, last = position()
    slot = plan[0, tick]
    stored = (stash.at[slot], bwd_routes_t.at[slot])
    mine = fwd_routes_t.at[tick]
    if odd_forward:
        ahead, behind = odd, even
        cases = [((odd,), act_in, mine), ((even,), *stored)]
        g_cases = [((even,), grad_in, None)]
    else:
        ahead, behind = even, odd
        cases = [
            ((first,), examples.at[tick], mine),
            ((even, jnp.logical_not(first)), act_in, mine),
            ((last,), act_in, mine),
            ((odd, jnp.logical_not(last)), *stored),
        ]
        g_cases = [
            ((last,), output, examples.at[tick]),
            ((odd, jnp.logical_not(last)), grad_in, None),
        ]
    x_wait = fetch(cases, x_s, b_s, r_s, sems)
    copies = fetch_weights(hbm, weights, FIRST_ORDER, sems)
    g_wait = fetch_cotangent(g_cases, g_s, e_s, sems)
    x_wait()
    values = primal_of(x_s[...], r_s[...], copies, weights)
    copies["down"].wait()

    @pl.when(ahead)
    def _():
        sent[...] = output_of(x_s, values, weights[6])

    @pl.when(behind)
    def _():
        g_wait()
        dx, ga, gb = gradients(x_s, g_s, values, weights)
        sent[...] = dx
        factor = normalizer(ga, gb, mean_scale)
        if tick:
            pack(packed, ga_in[...] + factor * ga, gb_in[...] + factor * gb)
        else:
            ga_out[...] = factor * ga
            gb_out[...] = factor * gb


def recompute_kernel(tick, plan, act_in, after, examples, stash, fwd_routes_t, bwd_routes_t, *rest):
    hbm, outs, (b_s, r_s, *weights, sems) = rest[:6], rest[6:13], rest[13:]
    x_o, rstd_o, normed_o, share_o, low_o, gate_o, up_o = outs
    odd, _, _, last = position()

    @pl.when(odd)
    def _():
        slot = plan[0, tick]
        cases = [
            ((last,), act_in, fwd_routes_t.at[tick]),
            ((jnp.logical_not(last),), stash.at[slot], bwd_routes_t.at[slot]),
        ]
        x_wait = fetch(cases, x_o, b_s, r_s, sems)
        copies = fetch_weights(hbm, weights, FIRST_ORDER[:6], sems)
        x_wait()
        values = primal_of(x_o[...], r_s[...], copies, weights)
        rstd, normed, share, _, low, gate_pre, up_pre = values
        rstd_o[...] = jnp.broadcast_to(rstd, rstd_o.shape)
        normed_o[...] = normed
        share_o[...] = share
        low_o[...] = low
        gate_o[...] = gate_pre
        up_o[...] = up_pre


def last_kernel(
    tick,
    mean_scale,
    arrived,
    output,
    examples,
    fwd_routes_t,
    packed_in,
    ga_in,
    gb_in,
    *rest,
):
    saved, rest = rest[:7], rest[7:]
    hbm, (sent, packed, x_s, g_s, b_s, e_s, r_s, *weights, sems) = rest[:7], rest[7:]
    x_o, rstd_o, normed_o, share_o, low_o, gate_o, up_o = saved
    odd, even, first, last = position()

    @pl.when(even)
    def _():
        keep = pltpu.make_async_copy(packed_in, packed, sems.at[2])
        keep.start()
        mine = fwd_routes_t.at[tick]
        cases = [
            ((first,), examples.at[tick], mine),
            ((jnp.logical_not(first),), arrived, mine),
        ]
        x_wait = fetch(cases, x_s, b_s, r_s, sems)
        copies = fetch_weights(hbm, weights, FIRST_ORDER, sems)
        x_wait()
        values = primal_of(x_s[...], r_s[...], copies, weights)
        copies["down"].wait()
        sent[...] = output_of(x_s, values, weights[6])
        keep.wait()

    @pl.when(odd)
    def _():
        g_cases = [
            ((last,), output, examples.at[tick]),
            ((jnp.logical_not(last),), arrived, None),
        ]
        g_wait = fetch_cotangent(g_cases, g_s, e_s, sems)
        copies = fetch_weights(hbm, weights, ("down", "b", "gate", "up", "router", "a", "gain"), sems)
        share = share_o[...]
        values = (
            rstd_o[:, 0:1],
            normed_o[...],
            share,
            share[:, 0:1],
            low_o[...],
            gate_o[...],
            up_o[...],
        )
        for name in NAMES:
            copies[name].wait()
        g_wait()
        dx, ga, gb = gradients(x_o, g_s, values, weights)
        sent[...] = dx
        factor = normalizer(ga, gb, mean_scale)
        pack(packed, ga_in[...] + factor * ga, gb_in[...] + factor * gb)


def sum_kernel(parts, total):
    total[...] = jnp.sum(parts[...], axis=0).reshape(total.shape)


def final_kernel(tall, half, pieces, parts, slow, fast, ga, gb, acts_o, grads_o, slow_s, fast_s, sems):
    odd, even, _, _ = position()
    rows = slow.shape[0] // pieces
    moves = []
    for source, stage, low, high in (
        (slow, slow_s, acts_o, grads_o),
        (fast, fast_s, grads_o, acts_o),
    ):
        for i in range(pieces):
            at = pl.ds(i * rows, rows)
            k = 2 * len(moves)
            move_in = pltpu.make_async_copy(source.at[at], stage.at[at], sems.at[k])
            move_even = pltpu.make_async_copy(stage.at[at], low.at[at], sems.at[k + 1])
            move_odd = pltpu.make_async_copy(stage.at[at], high.at[at], sems.at[k + 1])
            moves.append((move_in, move_even, move_odd))
    for move_in, _, _ in moves:
        move_in.start()
    for move_in, move_even, move_odd in moves:
        move_in.wait()
        pl.when(even)(move_even.start)
        pl.when(odd)(move_odd.start)
    total = jnp.sum(parts[...], axis=0)
    ga[...] = total[:tall]
    rank = gb.shape[2]
    for side in range(2):
        for part in range(2):
            lane = part * tall + side * rank
            gb[side, part * half : (part + 1) * half, :] = total[
                tall : tall + half, lane : lane + rank
            ]
    for _, move_even, move_odd in moves:
        pl.when(even)(move_even.wait)
        pl.when(odd)(move_odd.wait)


def swaps(first, count):
    pairs = []
    for s in range(first, count - 1, 2):
        pairs += [(s, s + 1), (s + 1, s)]
    return pairs


def shards(
    y_size,
    examples,
    arriving,
    returning,
    stash,
    plan,
    forward_expert_routes,
    backward_expert_routes,
    input_norm_gain,
    router,
    frozen_gate_weight,
    frozen_up_weight,
    frozen_down_weight,
    down_factors,
    up_factors,
):
    replicas = lax.axis_size("dp")
    z_size = replicas // y_size
    ticks, tokens, width = examples.shape
    mean_scale = 1.0 / (ticks * replicas)
    gain, router, gate, up, down = (
        input_norm_gain,
        router[0],
        frozen_gate_weight[0],
        frozen_up_weight[0],
        frozen_down_weight[0],
    )
    a_t = down_factors[0].T
    b = up_factors[0]
    stash = stash[0]
    fwd_routes_t = jnp.swapaxes(forward_expert_routes[0], 1, 2)
    bwd_routes_t = jnp.swapaxes(backward_expert_routes[0], 1, 2)
    topk = fwd_routes_t.shape[1]
    hidden_units = gate.shape[1]
    columns = a_t.shape[0]
    weights = (gain, router, a_t, gate, up, b, down)
    scratch = [pltpu.VMEM(w.shape, w.dtype) for w in weights]
    x_scratch = pltpu.VMEM((tokens, width), F32)
    b_scratch = pltpu.VMEM((tokens, width), BF16)
    r_scratch = pltpu.VMEM((topk, tokens), jnp.int32)
    semaphores = pltpu.SemaphoreType.DMA((12,))
    activation = jax.ShapeDtypeStruct((tokens, width), F32)
    adapter_a = jax.ShapeDtypeStruct((columns, width), F32)
    adapter_b = jax.ShapeDtypeStruct((columns, hidden_units), F32)
    whole = pltpu.CompilerParams()
    some = pltpu.CompilerParams(vmem_limit_bytes=24 << 20)
    few = pltpu.CompilerParams(vmem_limit_bytes=8 << 20)
    primal_flops = 2 * tokens * width * (router.shape[1] + columns + 2 * hidden_units)
    down_flops = 2 * tokens * width * hidden_units
    weight_bytes = sum(w.size * w.dtype.itemsize for w in weights)

    def cost(flops):
        return pl.CostEstimate(
            flops=flops, bytes_accessed=weight_bytes + 8 * tokens * width, transcendentals=0
        )

    sections = lax.axis_size("section")
    near = swaps(0, sections)
    far = swaps(1, sections)
    rows_each = hidden_units // replicas
    size = columns + -(-(rows_each // 2) // 8) * 8
    share_width = width // replicas
    packed_shape = jax.ShapeDtypeStruct((y_size, z_size * size, share_width), F32)
    work = [x_scratch, x_scratch, b_scratch, b_scratch, r_scratch, *scratch, semaphores]

    def step(tick, odd_forward, acts, grads, output, sums, params):
        outs = (activation, packed_shape) if tick else (activation, adapter_a, adapter_b)
        return pl.pallas_call(
            functools.partial(step_kernel, tick, odd_forward, mean_scale),
            out_shape=outs,
            in_specs=[SMEM] + [ANY] * (7 + len(weights)) + [VMEM] * len(sums),
            out_specs=(VMEM,) * len(outs),
            scratch_shapes=work,
            compiler_params=params,
            cost_estimate=cost(2 * primal_flops + down_flops),
        )(plan, acts, grads, output, examples, stash, fwd_routes_t, bwd_routes_t, *weights, *sums)

    start = arriving[0]
    back = returning[0]
    sent, *even_sums = step(0, True, start, back, start, (), whole)
    slow_0 = lax.ppermute(sent, "section", far)
    sent, *odd_sums = step(0, False, start, back, sent, (), whole)
    fast_0 = lax.ppermute(sent, "section", near)
    ahead, packed = step(1, True, fast_0, fast_0, fast_0, even_sums, whole)
    slow_1 = lax.ppermute(ahead, "section", far)
    saved = pl.pallas_call(
        functools.partial(recompute_kernel, 1),
        out_shape=(
            activation,
            jax.ShapeDtypeStruct((tokens, 128), F32),
            jax.ShapeDtypeStruct((tokens, width), BF16),
            jax.ShapeDtypeStruct((tokens, router.shape[1]), F32),
            jax.ShapeDtypeStruct((tokens, columns), BF16),
            jax.ShapeDtypeStruct((tokens, hidden_units), F32),
            jax.ShapeDtypeStruct((tokens, hidden_units), F32),
        ),
        in_specs=[SMEM] + [ANY] * (6 + len(weights) - 1),
        out_specs=(VMEM,) * 7,
        scratch_shapes=[b_scratch, r_scratch, *scratch[:-1], semaphores],
        compiler_params=some,
        cost_estimate=cost(primal_flops),
        name="recompute_1",
    )(plan, fast_0, ahead, examples, stash, fwd_routes_t, bwd_routes_t, *weights[:-1])
    sent, packed = pl.pallas_call(
        functools.partial(last_kernel, 1, mean_scale),
        out_shape=(activation, packed_shape),
        in_specs=[ANY] * 5 + [VMEM] * 2 + [VMEM] * len(saved) + [ANY] * len(weights),
        out_specs=(VMEM,) * 2,
        scratch_shapes=work,
        compiler_params=some,
        cost_estimate=cost(primal_flops + down_flops),
        name="step_1b",
    )(slow_0, ahead, examples, fwd_routes_t, packed, *odd_sums, *saved, *weights)
    fast_1 = lax.ppermute(sent, "section", near)
    y_groups = [[z * y_size + y for y in range(y_size)] for z in range(z_size)]
    z_groups = [[z * y_size + y for z in range(z_size)] for y in range(y_size)]
    parts = lax.all_to_all(packed, "dp", 0, 0, axis_index_groups=y_groups, tiled=True)
    parts = pl.pallas_call(
        sum_kernel,
        out_shape=jax.ShapeDtypeStruct((z_size, size, share_width), F32),
        in_specs=[VMEM],
        out_specs=VMEM,
        compiler_params=few,
        name="sum_y",
    )(parts)
    parts = lax.all_to_all(parts, "dp", 0, 0, axis_index_groups=z_groups, tiled=True)
    pieces = 4
    share_a, share_b, next_acts, next_grads = pl.pallas_call(
        functools.partial(final_kernel, columns, rows_each // 2, pieces),
        out_shape=(
            jax.ShapeDtypeStruct((columns, share_width), F32),
            jax.ShapeDtypeStruct((2, rows_each, columns // 2), F32),
            activation,
            activation,
        ),
        in_specs=[VMEM, ANY, ANY],
        out_specs=(VMEM, VMEM, ANY, ANY),
        scratch_shapes=[x_scratch, x_scratch, pltpu.SemaphoreType.DMA((4 * pieces,))],
        compiler_params=few,
        name="sum_z",
    )(parts, slow_1, fast_1)
    return (
        next_acts[None],
        next_grads[None],
        share_a.T[None],
        jnp.swapaxes(share_b, 1, 2)[None],
    )


def solution(mesh):
    in_specs = (
        P(None, "dp", None),
        P("section", "dp", None),
        P("section", "dp", None),
        P("section", None, "dp", None),
        P("section", None),
        P("section", None, "dp", None),
        P("section", None, "dp", None),
        P("section", None),
        P("section", None, None),
        P("section", None, None),
        P("section", None, None),
        P("section", None, None),
        P("section", None, None),
        P("section", None, None, None),
    )
    out_specs = (
        P("section", "dp", None),
        P("section", "dp", None),
        P("section", "dp", None),
        P("section", None, None, "dp"),
    )

    def body(*args):
        return shards(4, *args)

    return jax.shard_map(
        body, mesh=mesh, in_specs=in_specs, out_specs=out_specs, check_vma=False
    )
```

```python
import functools

import jax
import jax.numpy as jnp
from jax import lax
from jax.experimental import pallas as pl
from jax.experimental.pallas import tpu as pltpu
from jax.sharding import PartitionSpec as P


SCALE = 2.0
EPS = 1e-06
F32 = jnp.float32
BF16 = jnp.bfloat16
ANY = pl.BlockSpec(memory_space=pl.ANY)
SMEM = pl.BlockSpec(memory_space=pltpu.SMEM)
VMEM = pl.BlockSpec(memory_space=pltpu.VMEM)


def nn(a, b):
    return jnp.dot(a, b, preferred_element_type=F32)


def nt(a, b):
    return lax.dot_general(a, b, (((1,), (1,)), ((), ())), preferred_element_type=F32)


def primal(x, routes_t, gain, copies, router, a_t, gate, up, factors):
    def ready(name):
        if copies is not None:
            copies[name].wait()

    rstd = lax.rsqrt(jnp.mean(x * x, axis=-1, keepdims=True) + EPS)
    normed = (x * rstd * gain).astype(BF16)
    ready("router")
    logits = nn(normed, router[...])
    experts = logits.shape[1]
    expert = lax.broadcasted_iota(jnp.int32, (experts, routes_t.shape[1]), 0)
    named = jnp.zeros(expert.shape, F32)
    for k in range(routes_t.shape[0]):
        named = jnp.where(routes_t[k : k + 1, :] == expert, 1.0, named)
    scores = jnp.where(named.T > 0.5, jnp.exp(logits), 0.0)
    share = scores / jnp.sum(scores, axis=-1, keepdims=True)
    weight = share[:, 0:1]
    ready("a")
    low = nt(normed, a_t[...]).astype(BF16)
    rank = low.shape[1] // 2
    ready("b")
    ready("gate")
    gate_pre = nn(normed, gate[...]) + SCALE * nn(low[:, :rank], factors[0])
    ready("up")
    up_pre = nn(normed, up[...]) + SCALE * nn(low[:, rank:], factors[1])
    return rstd, normed, share, weight, low, gate_pre, up_pre


def when_all(*predicates):
    both = predicates[0]
    for predicate in predicates[1:]:
        both = jnp.logical_and(both, predicate)
    return pl.when(both)


def position():
    section = lax.axis_index("section")
    odd = lax.rem(section, 2) == 1
    return (
        odd,
        jnp.logical_not(odd),
        section == 0,
        section == lax.axis_size("section") - 1,
    )


def fetch(cases, x_s, b_s, r_s, sems):
    moves = []
    for predicates, source, routes in cases:
        narrow = source.dtype == BF16
        mine = [pltpu.make_async_copy(source, b_s if narrow else x_s, sems.at[0])]
        if routes is not None:
            mine.append(pltpu.make_async_copy(routes, r_s, sems.at[1]))
        moves.append((predicates, narrow, mine))

        @when_all(*predicates)
        def _(mine=mine):
            for copy in mine:
                copy.start()

    def wait():
        for predicates, narrow, mine in moves:

            @when_all(*predicates)
            def _(narrow=narrow, mine=mine):
                for copy in mine:
                    copy.wait()
                if narrow:
                    x_s[...] = b_s[...].astype(F32)

    return wait


NAMES = ("gain", "router", "a", "gate", "up", "b", "down")


def fetch_weights(hbm, weights, order, sems):
    copies = {}
    for name in order:
        i = NAMES.index(name)
        copies[name] = pltpu.make_async_copy(hbm[i], weights[i], sems.at[i])
        copies[name].start()
    return copies


def primal_of(x, routes, copies, weights):
    gain_s, router, a_t, gate, up, factors = weights[:6]
    if copies is not None:
        copies["gain"].wait()
    return primal(x, routes, gain_s[...], copies, router, a_t, gate, up, factors)


def output_of(x_s, values, down):
    _, _, _, weight, _, gate_pre, up_pre = values
    hidden = (gate_pre * jax.nn.sigmoid(gate_pre) * up_pre).astype(BF16)
    return x_s[...] + weight * nn(hidden, down[...])


def gradients(x_s, g_s, saved, weights, copies=None, x_wait=None):
    def ready(*names):
        if copies is not None:
            for name in names:
                copies[name].wait()

    gain_s, router, a_t, gate, up, factors, down = weights
    rstd, normed, share, weight, low, gate_pre, up_pre = saved
    sig = jax.nn.sigmoid(gate_pre)
    silu = gate_pre * sig
    hidden = (silu * up_pre).astype(BF16)
    ready("down")
    back = nt(g_s[...].astype(BF16), down[...])
    d_weight = jnp.sum(hidden.astype(F32) * back, axis=-1, keepdims=True)
    lead = (lax.broadcasted_iota(jnp.int32, share.shape, 1) == 0).astype(F32)
    d_logits = ((d_weight * weight) * (lead - share)).astype(BF16)
    d_hidden = (weight * back).astype(BF16).astype(F32)
    d_gate = (d_hidden * up_pre * (sig * (1.0 + gate_pre * (1.0 - sig)))).astype(BF16)
    d_up = (d_hidden * silu).astype(BF16)
    ready("b", "gate", "up", "router", "a", "gain")
    if x_wait is not None:
        x_wait()
    d_low_f = SCALE * jnp.concatenate([nt(d_gate, factors[0]), nt(d_up, factors[1])], axis=1)
    d_normed = (
        nt(d_gate, gate[...])
        + nt(d_up, up[...])
        + nt(d_logits, router[...])
        + nn(d_low_f.astype(BF16), a_t[...])
    )
    scaled = d_normed * gain_s[...]
    x = x_s[...]
    along = jnp.mean(scaled * x, axis=-1, keepdims=True) * (rstd * rstd)
    dx = g_s[...] + rstd * (scaled - x * along)
    rank = low.shape[1] // 2
    ga = nn(d_low_f.T.astype(BF16), normed)
    low_t = low.astype(F32).T.astype(BF16)
    gb = SCALE * jnp.concatenate([nn(low_t[:rank], d_gate), nn(low_t[rank:], d_up)], axis=0)
    return dx, ga, gb


def normalizer(ga, gb, mean_scale):
    square = (jnp.sum(ga * ga) + jnp.sum(gb * gb)) / (ga.size + gb.size)
    return lax.rsqrt(square + EPS) * mean_scale


def pack(packed, ga, gb):
    gb_t = gb.T
    parts, size, width = packed.shape
    rows = gb_t.shape[0] // parts
    tall = ga.shape[0]
    half = rows // 2
    for p in range(parts):
        packed[p, :tall, :] = ga[:, p * width : (p + 1) * width]
        packed[p, tall : tall + half, :tall] = gb_t[p * rows : p * rows + half]
        packed[p, tall : tall + half, tall:] = gb_t[p * rows + half : (p + 1) * rows]
        packed[p, tall + half :, :] = jnp.zeros((size - tall - half, width), F32)


FIRST_ORDER = ("gain", "router", "a", "b", "gate", "up", "down")
X1, X2, G, W, OUT = (pl.ds(0, 2), pl.ds(2, 2), pl.ds(4, 2), pl.ds(6, 7), pl.ds(13, 7))


def first_kernel(
    mean_scale, plan, arriving, returning, examples, stash, fwd_routes_t, bwd_routes_t, *rest
):
    hbm, (slow_o, fast_o, ga_o, gb_o), rest = rest[:7], rest[7:11], rest[11:]
    x_s, x2_s, g_s, y_s, d_s, b_s, b2_s, e_s, r_s, r2_s, ga_s, gb_s, *weights, sems = rest
    odd, even, first, last = position()
    slot = plan[0, 0]
    mine = fwd_routes_t.at[0]
    x_wait = fetch(
        [
            ((first,), examples.at[0], mine),
            ((jnp.logical_not(first),), arriving, mine),
        ],
        x_s,
        b_s,
        r_s,
        sems.at[X1],
    )
    copies = fetch_weights(hbm, weights, FIRST_ORDER, sems.at[W])
    x2_wait = fetch(
        [
            ((last,), arriving, mine),
            ((jnp.logical_not(last),), stash.at[slot], bwd_routes_t.at[slot]),
        ],
        x2_s,
        b2_s,
        r2_s,
        sems.at[X2],
    )
    g_copy = pltpu.make_async_copy(returning, g_s, sems.at[4])
    t_copy = pltpu.make_async_copy(examples.at[0], e_s, sems.at[5])
    pl.when(jnp.logical_not(last))(g_copy.start)
    pl.when(last)(t_copy.start)
    x_wait()
    values = primal_of(x_s[...], r_s[...], copies, weights)
    copies["down"].wait()
    y_s[...] = output_of(x_s, values, weights[6])
    outs = sems.at[OUT]
    y_slow = pltpu.make_async_copy(y_s, slow_o, outs.at[0])
    y_fast = pltpu.make_async_copy(y_s, fast_o, outs.at[0])
    d_slow = pltpu.make_async_copy(d_s, slow_o, outs.at[1])
    d_fast = pltpu.make_async_copy(d_s, fast_o, outs.at[1])
    pl.when(odd)(y_slow.start)
    pl.when(even)(y_fast.start)
    x2_wait()

    @pl.when(last)
    def _():
        t_copy.wait()
        g_s[...] = y_s[...] - e_s[...].astype(F32)

    values = primal_of(x2_s[...], r2_s[...], None, weights)
    pl.when(jnp.logical_not(last))(g_copy.wait)
    dx, ga, gb = gradients(x2_s, g_s, values, weights)
    d_s[...] = dx
    pl.when(odd)(d_fast.start)
    pl.when(even)(d_slow.start)
    factor = normalizer(ga, gb, mean_scale)
    ga_s[...] = factor * ga
    gb_s[...] = factor * gb
    tail = [
        pltpu.make_async_copy(ga_s, ga_o, outs.at[2]),
        pltpu.make_async_copy(gb_s, gb_o, outs.at[3]),
    ]
    for copy in tail:
        copy.start()
    for copy in tail:
        copy.wait()

    @pl.when(odd)
    def _():
        y_slow.wait()
        d_fast.wait()

    @pl.when(even)
    def _():
        y_fast.wait()
        d_slow.wait()


def second_kernel(
    tick, mean_scale, plan, arrived, stash, fwd_routes_t, bwd_routes_t, ga_in, gb_in, *rest
):
    hbm, (sent, packed, *saved_o), rest = rest[:7], rest[7:15], rest[15:]
    x_s, x2_s, y_s, b_s, b2_s, r_s, r2_s, ga_s, gb_s, packed_s, *rest = rest
    saved, weights, sems = rest[:6], rest[6:13], rest[13]
    odd, even, _, last = position()
    slot = plan[0, tick]
    mine = fwd_routes_t.at[tick]
    stored = (stash.at[slot], bwd_routes_t.at[slot])
    inner = jnp.logical_and(odd, jnp.logical_not(last))
    x_wait = fetch([((odd,), arrived, mine), ((even,), *stored)], x_s, b_s, r_s, sems.at[X1])
    copies = fetch_weights(hbm, weights, FIRST_ORDER, sems.at[W])
    x2_wait = fetch(
        [((last,), arrived, mine), ((inner,), *stored)], x2_s, b2_s, r2_s, sems.at[X2]
    )
    g_copies = [
        pltpu.make_async_copy(arrived, x2_s, sems.at[4]),
        pltpu.make_async_copy(ga_in, ga_s, sems.at[5]),
        pltpu.make_async_copy(gb_in, gb_s, sems.at[20]),
    ]

    @pl.when(even)
    def _():
        for copy in g_copies:
            copy.start()

    x_wait()
    values = primal_of(x_s[...], r_s[...], copies, weights)
    copies["down"].wait()
    outs = sems.at[OUT]
    y_copy = pltpu.make_async_copy(y_s, sent, outs.at[0])

    @pl.when(odd)
    def _():
        y_s[...] = output_of(x_s, values, weights[6])
        y_copy.start()
        x2_wait()
        rstd, normed, share, _, low, gate_pre, up_pre = primal_of(
            x2_s[...], r2_s[...], None, weights
        )
        kept = (jnp.broadcast_to(rstd, saved[0].shape), normed, share, low, gate_pre, up_pre)
        moves = []
        for i, value in enumerate(kept):
            saved[i][...] = value
            moves.append(pltpu.make_async_copy(saved[i], saved_o[i], outs.at[1 + i]))
            moves[-1].start()
        for move in moves:
            move.wait()

    @pl.when(even)
    def _():
        for copy in g_copies:
            copy.wait()
        dx, ga, gb = gradients(x_s, x2_s, values, weights)
        y_s[...] = dx
        y_copy.start()
        factor = normalizer(ga, gb, mean_scale)
        pack(packed_s, ga_s[...] + factor * ga, gb_s[...] + factor * gb)
        move = pltpu.make_async_copy(packed_s, packed, outs.at[1])
        move.start()
        move.wait()

    y_copy.wait()


def third_kernel(
    tick,
    mean_scale,
    plan,
    arrived,
    near,
    output,
    examples,
    stash,
    fwd_routes_t,
    packed_in,
    ga_in,
    gb_in,
    *rest,
):
    saved_in, rest = rest[:6], rest[6:]
    hbm, (sent, packed), rest = rest[:7], rest[7:9], rest[9:]
    x_s, g_s, y_s, b_s, e_s, r_s, ga_s, gb_s, packed_s, *rest = rest
    saved, weights, sems = rest[:6], rest[6:13], rest[13]
    odd, even, first, last = position()
    inner = jnp.logical_and(odd, jnp.logical_not(last))
    outs = sems.at[OUT]
    y_copy = pltpu.make_async_copy(y_s, sent, outs.at[0])
    p_copy = pltpu.make_async_copy(packed_s, packed, outs.at[1])

    @pl.when(even)
    def _():
        mine = fwd_routes_t.at[tick]
        x_wait = fetch(
            [
                ((first,), examples.at[tick], mine),
                ((jnp.logical_not(first),), arrived, mine),
            ],
            x_s,
            b_s,
            r_s,
            sems.at[X1],
        )
        copies = fetch_weights(hbm, weights, FIRST_ORDER, sems.at[W])
        keep = pltpu.make_async_copy(packed_in, packed_s, sems.at[4])
        keep.start()
        x_wait()
        values = primal_of(x_s[...], r_s[...], copies, weights)
        copies["down"].wait()
        keep.wait()
        p_copy.start()
        y_s[...] = output_of(x_s, values, weights[6])
        y_copy.start()

    @pl.when(odd)
    def _():
        g_copy = pltpu.make_async_copy(arrived, g_s, sems.at[4])
        o_copy = pltpu.make_async_copy(output, g_s, sems.at[4])
        t_copy = pltpu.make_async_copy(examples.at[tick], e_s, sems.at[5])
        pl.when(inner)(g_copy.start)

        @pl.when(last)
        def _():
            o_copy.start()
            t_copy.start()

        moves = [pltpu.make_async_copy(saved_in[i], saved[i], outs.at[1 + i]) for i in range(6)]
        for i in (2, 4, 5):
            moves[i].start()
        copies = fetch_weights(hbm, weights, ("down", "b", "gate", "up"), sems.at[W])
        for i in (0, 1, 3):
            moves[i].start()
        x_wait = fetch(
            [((last,), near, None), ((inner,), stash.at[plan[0, tick]], None)],
            x_s,
            b_s,
            None,
            sems.at[X1],
        )
        copies.update(fetch_weights(hbm, weights, ("router", "a", "gain"), sems.at[W]))
        sums = [
            pltpu.make_async_copy(ga_in, ga_s, sems.at[2]),
            pltpu.make_async_copy(gb_in, gb_s, sems.at[3]),
        ]
        for copy in sums:
            copy.start()
        for move in moves:
            move.wait()
        pl.when(inner)(g_copy.wait)

        @pl.when(last)
        def _():
            o_copy.wait()
            t_copy.wait()
            g_s[...] = g_s[...] - e_s[...].astype(F32)

        rstd, normed, share, low, gate_pre, up_pre = (ref[...] for ref in saved)
        values = (rstd[:, 0:1], normed, share, share[:, 0:1], low, gate_pre, up_pre)
        dx, ga, gb = gradients(x_s, g_s, values, weights, copies, x_wait)
        y_s[...] = dx
        y_copy.start()
        factor = normalizer(ga, gb, mean_scale)
        for copy in sums:
            copy.wait()
        pack(packed_s, ga_s[...] + factor * ga, gb_s[...] + factor * gb)
        p_copy.start()

    y_copy.wait()
    p_copy.wait()


def final_kernel(tall, half, pieces, parts, slow, fast, ga, gb, acts_o, grads_o, slow_s, fast_s, sems):
    odd, even, _, _ = position()
    rows = slow.shape[0] // pieces
    moves = []
    for source, stage, low, high in (
        (slow, slow_s, acts_o, grads_o),
        (fast, fast_s, grads_o, acts_o),
    ):
        for i in range(pieces):
            at = pl.ds(i * rows, rows)
            k = 2 * len(moves)
            move_in = pltpu.make_async_copy(source.at[at], stage.at[at], sems.at[k])
            move_even = pltpu.make_async_copy(stage.at[at], low.at[at], sems.at[k + 1])
            move_odd = pltpu.make_async_copy(stage.at[at], high.at[at], sems.at[k + 1])
            moves.append((move_in, move_even, move_odd))
    for move_in, _, _ in moves:
        move_in.start()
    for move_in, move_even, move_odd in moves:
        move_in.wait()
        pl.when(even)(move_even.start)
        pl.when(odd)(move_odd.start)
    total = jnp.sum(parts[...], axis=0)
    ga[...] = total[:tall]
    rank = gb.shape[2]
    for side in range(2):
        for part in range(2):
            lane = part * tall + side * rank
            gb[side, part * half : (part + 1) * half, :] = total[
                tall : tall + half, lane : lane + rank
            ]
    for _, move_even, move_odd in moves:
        pl.when(even)(move_even.wait)
        pl.when(odd)(move_odd.wait)


def swaps(first, count):
    pairs = []
    for s in range(first, count - 1, 2):
        pairs += [(s, s + 1), (s + 1, s)]
    return pairs


def shards(
    examples,
    arriving,
    returning,
    stash,
    plan,
    forward_expert_routes,
    backward_expert_routes,
    input_norm_gain,
    router,
    frozen_gate_weight,
    frozen_up_weight,
    frozen_down_weight,
    down_factors,
    up_factors,
):
    replicas = lax.axis_size("dp")
    ticks, tokens, width = examples.shape
    mean_scale = 1.0 / (ticks * replicas)
    gain, router, gate, up, down = (
        input_norm_gain,
        router[0],
        frozen_gate_weight[0],
        frozen_up_weight[0],
        frozen_down_weight[0],
    )
    a_t = down_factors[0].T
    b = up_factors[0]
    stash = stash[0]
    fwd_routes_t = jnp.swapaxes(forward_expert_routes[0], 1, 2)
    bwd_routes_t = jnp.swapaxes(backward_expert_routes[0], 1, 2)
    topk = fwd_routes_t.shape[1]
    hidden_units = gate.shape[1]
    columns = a_t.shape[0]
    weights = (gain, router, a_t, gate, up, b, down)
    scratch = [pltpu.VMEM(w.shape, w.dtype) for w in weights]
    x_scratch = pltpu.VMEM((tokens, width), F32)
    b_scratch = pltpu.VMEM((tokens, width), BF16)
    r_scratch = pltpu.VMEM((topk, tokens), jnp.int32)
    semaphores = pltpu.SemaphoreType.DMA((21,))
    sections = lax.axis_size("section")
    near = swaps(0, sections)
    far = swaps(1, sections)
    rows_each = hidden_units // replicas
    size = columns + -(-(rows_each // 2) // 8) * 8
    share_width = width // replicas
    activation = jax.ShapeDtypeStruct((tokens, width), F32)
    sums_shape = (
        jax.ShapeDtypeStruct((columns, width), F32),
        jax.ShapeDtypeStruct((columns, hidden_units), F32),
    )
    packed_shape = jax.ShapeDtypeStruct((replicas, size, share_width), F32)
    saved_shape = (
        jax.ShapeDtypeStruct((tokens, 128), F32),
        jax.ShapeDtypeStruct((tokens, width), BF16),
        jax.ShapeDtypeStruct((tokens, router.shape[1]), F32),
        jax.ShapeDtypeStruct((tokens, columns), BF16),
        jax.ShapeDtypeStruct((tokens, hidden_units), F32),
        jax.ShapeDtypeStruct((tokens, hidden_units), F32),
    )

    def rooms(shapes):
        return [pltpu.VMEM(shape.shape, shape.dtype) for shape in shapes]

    primal_flops = 2 * tokens * width * (router.shape[1] + columns + 2 * hidden_units)
    down_flops = 2 * tokens * width * hidden_units
    weight_bytes = sum(w.size * w.dtype.itemsize for w in weights)

    def kernel(body, flops, outs, rooms, operands):
        return pl.pallas_call(
            body,
            out_shape=outs,
            in_specs=[SMEM] + [ANY] * (len(operands) - 1),
            out_specs=(ANY,) * len(outs),
            scratch_shapes=[*rooms, *scratch, semaphores],
            cost_estimate=pl.CostEstimate(
                flops=flops, bytes_accessed=weight_bytes + 8 * tokens * width, transcendentals=0
            ),
        )(*operands)

    slow, fast, *sums = kernel(
        functools.partial(first_kernel, mean_scale),
        3 * primal_flops + 2 * down_flops,
        (activation, activation, *sums_shape),
        [x_scratch] * 5 + [b_scratch] * 3 + [r_scratch] * 2 + rooms(sums_shape),
        (plan, arriving[0], returning[0], examples, stash, fwd_routes_t, bwd_routes_t, *weights),
    )
    slow_0 = lax.ppermute(slow, "section", far)
    fast_0 = lax.ppermute(fast, "section", near)
    ahead, packed, *saved = kernel(
        functools.partial(second_kernel, 1, mean_scale),
        2 * primal_flops + down_flops,
        (activation, packed_shape, *saved_shape),
        [x_scratch] * 3
        + [b_scratch] * 2
        + [r_scratch] * 2
        + rooms((*sums_shape, packed_shape, *saved_shape)),
        (plan, fast_0, stash, fwd_routes_t, bwd_routes_t, *sums, *weights),
    )
    slow_1 = lax.ppermute(ahead, "section", far)
    sent, packed = kernel(
        functools.partial(third_kernel, 1, mean_scale),
        primal_flops + down_flops,
        (activation, packed_shape),
        [x_scratch] * 3
        + [b_scratch] * 2
        + [r_scratch]
        + rooms((*sums_shape, packed_shape, *saved_shape)),
        (plan, slow_0, fast_0, ahead, examples, stash, fwd_routes_t, packed, *sums, *saved, *weights),
    )
    parts = lax.all_to_all(packed, "dp", 0, 0, tiled=True)
    fast_1 = lax.ppermute(sent, "section", near)
    pieces = 4
    share_a, share_b, next_acts, next_grads = pl.pallas_call(
        functools.partial(final_kernel, columns, rows_each // 2, pieces),
        out_shape=(
            jax.ShapeDtypeStruct((columns, share_width), F32),
            jax.ShapeDtypeStruct((2, rows_each, columns // 2), F32),
            activation,
            activation,
        ),
        in_specs=[VMEM, ANY, ANY],
        out_specs=(VMEM, VMEM, ANY, ANY),
        scratch_shapes=[x_scratch, x_scratch, pltpu.SemaphoreType.DMA((4 * pieces,))],
        compiler_params=pltpu.CompilerParams(vmem_limit_bytes=8 << 20),
        name="sum_dp",
    )(parts, slow_1, fast_1)
    return (
        next_acts[None],
        next_grads[None],
        share_a.T[None],
        jnp.swapaxes(share_b, 1, 2)[None],
    )


def solution(mesh):
    in_specs = (
        P(None, "dp", None),
        P("section", "dp", None),
        P("section", "dp", None),
        P("section", None, "dp", None),
        P("section", None),
        P("section", None, "dp", None),
        P("section", None, "dp", None),
        P("section", None),
        P("section", None, None),
        P("section", None, None),
        P("section", None, None),
        P("section", None, None),
        P("section", None, None),
        P("section", None, None, None),
    )
    out_specs = (
        P("section", "dp", None),
        P("section", "dp", None),
        P("section", "dp", None),
        P("section", None, None, "dp"),
    )

    return jax.shard_map(shards, mesh=mesh, in_specs=in_specs, out_specs=out_specs, check_vma=False)
```

```python
import functools

import jax
import jax.numpy as jnp
from jax import lax
from jax.experimental import pallas as pl
from jax.experimental.pallas import tpu as pltpu
from jax.sharding import PartitionSpec as P


SCALE = 2.0
EPS = 1e-06
F32 = jnp.float32
BF16 = jnp.bfloat16
ANY = pl.BlockSpec(memory_space=pl.ANY)
SMEM = pl.BlockSpec(memory_space=pltpu.SMEM)
VMEM = pl.BlockSpec(memory_space=pltpu.VMEM)


def nn(a, b):
    return jnp.dot(a, b, preferred_element_type=F32)


def nt(a, b):
    return lax.dot_general(a, b, (((1,), (1,)), ((), ())), preferred_element_type=F32)


def primal(x, routes_t, gain, copies, router, a_t, gate, up, factors):
    def ready(name):
        if copies is not None:
            copies[name].wait()

    rstd = lax.rsqrt(jnp.mean(x * x, axis=-1, keepdims=True) + EPS)
    normed = (x * rstd * gain).astype(BF16)
    ready("router")
    logits = nn(normed, router[...])
    experts = logits.shape[1]
    expert = lax.broadcasted_iota(jnp.int32, (experts, routes_t.shape[1]), 0)
    named = jnp.zeros(expert.shape, F32)
    for k in range(routes_t.shape[0]):
        named = jnp.where(routes_t[k : k + 1, :] == expert, 1.0, named)
    scores = jnp.where(named.T > 0.5, jnp.exp(logits), 0.0)
    share = scores / jnp.sum(scores, axis=-1, keepdims=True)
    weight = share[:, 0:1]
    ready("a")
    low = nt(normed, a_t[...]).astype(BF16)
    rank = low.shape[1] // 2
    ready("b")
    ready("gate")
    gate_pre = nn(normed, gate[...]) + SCALE * nn(low[:, :rank], factors[0])
    ready("up")
    up_pre = nn(normed, up[...]) + SCALE * nn(low[:, rank:], factors[1])
    return rstd, normed, share, weight, low, gate_pre, up_pre


def when_all(*predicates):
    both = predicates[0]
    for predicate in predicates[1:]:
        both = jnp.logical_and(both, predicate)
    return pl.when(both)


def position():
    section = lax.axis_index("section")
    odd = lax.rem(section, 2) == 1
    return (
        odd,
        jnp.logical_not(odd),
        section == 0,
        section == lax.axis_size("section") - 1,
    )


def fetch(cases, x_s, b_s, r_s, sems):
    moves = []
    for predicates, source, routes in cases:
        narrow = source.dtype == BF16
        mine = [pltpu.make_async_copy(source, b_s if narrow else x_s, sems.at[0])]
        if routes is not None:
            mine.append(pltpu.make_async_copy(routes, r_s, sems.at[1]))
        moves.append((predicates, narrow, mine))

        @when_all(*predicates)
        def _(mine=mine):
            for copy in mine:
                copy.start()

    def wait():
        for predicates, narrow, mine in moves:

            @when_all(*predicates)
            def _(narrow=narrow, mine=mine):
                for copy in mine:
                    copy.wait()
                if narrow:
                    x_s[...] = b_s[...].astype(F32)

    return wait


NAMES = ("gain", "router", "a", "gate", "up", "b", "down")


def fetch_weights(hbm, weights, order, sems):
    copies = {}
    for name in order:
        i = NAMES.index(name)
        copies[name] = pltpu.make_async_copy(hbm[i], weights[i], sems.at[i])
        copies[name].start()
    return copies


SOON = ("gain", "router", "a", "b", "gate")
THEN = ("up", "down")


def primal_of(x, routes, copies, weights):
    gain_s, router, a_t, gate, up, factors = weights[:6]
    if copies is not None:
        copies["gain"].wait()
    return primal(x, routes, gain_s[...], copies, router, a_t, gate, up, factors)


def output_of(x_s, values, down):
    _, _, _, weight, _, gate_pre, up_pre = values
    hidden = (gate_pre * jax.nn.sigmoid(gate_pre) * up_pre).astype(BF16)
    return x_s[...] + weight * nn(hidden, down[...])


def gradients(x_s, g_s, saved, weights, copies=None, late=None):
    def ready(*names):
        if copies is not None:
            for name in names:
                copies[name].wait()

    gain_s, router, a_t, gate, up, factors, down = weights
    if late is None:
        rstd, normed, share, weight, low, gate_pre, up_pre = saved
    else:
        share, gate_pre, up_pre = (saved[i][...] for i in (2, 4, 5))
        weight = share[:, 0:1]
    sig = jax.nn.sigmoid(gate_pre)
    silu = gate_pre * sig
    hidden = (silu * up_pre).astype(BF16)
    ready("down")
    back = nt(g_s[...].astype(BF16), down[...])
    d_weight = jnp.sum(hidden.astype(F32) * back, axis=-1, keepdims=True)
    lead = (lax.broadcasted_iota(jnp.int32, share.shape, 1) == 0).astype(F32)
    d_logits = ((d_weight * weight) * (lead - share)).astype(BF16)
    d_hidden = (weight * back).astype(BF16).astype(F32)
    d_gate = (d_hidden * up_pre * (sig * (1.0 + gate_pre * (1.0 - sig)))).astype(BF16)
    d_up = (d_hidden * silu).astype(BF16)
    ready("b", "gate", "up", "router", "a", "gain")
    if late is not None:
        rstd, normed, low = late()
    d_low_f = SCALE * jnp.concatenate([nt(d_gate, factors[0]), nt(d_up, factors[1])], axis=1)
    d_normed = (
        nt(d_gate, gate[...])
        + nt(d_up, up[...])
        + nt(d_logits, router[...])
        + nn(d_low_f.astype(BF16), a_t[...])
    )
    scaled = d_normed * gain_s[...]
    x = x_s[...]
    along = jnp.mean(scaled * x, axis=-1, keepdims=True) * (rstd * rstd)
    dx = g_s[...] + rstd * (scaled - x * along)
    rank = low.shape[1] // 2
    ga = nn(d_low_f.T.astype(BF16), normed)
    low_t = low.astype(F32).T.astype(BF16)
    gb = SCALE * jnp.concatenate([nn(low_t[:rank], d_gate), nn(low_t[rank:], d_up)], axis=0)
    return dx, ga, gb


def normalizer(ga, gb, mean_scale):
    square = (jnp.sum(ga * ga) + jnp.sum(gb * gb)) / (ga.size + gb.size)
    return lax.rsqrt(square + EPS) * mean_scale


def pack(packed, ga, gb):
    gb_t = gb.T
    ys, _, width = packed.shape
    zs = ga.shape[1] // (ys * width)
    size = packed.shape[1] // zs
    rows = gb_t.shape[0] // (ys * zs)
    tall = ga.shape[0]
    half = rows // 2
    for y in range(ys):
        for z in range(zs):
            p = z * ys + y
            at = z * size
            packed[y, at : at + tall, :] = ga[:, p * width : (p + 1) * width]
            at += tall
            packed[y, at : at + half, :tall] = gb_t[p * rows : p * rows + half]
            packed[y, at : at + half, tall:] = gb_t[p * rows + half : (p + 1) * rows]
            packed[y, at + half : (z + 1) * size, :] = jnp.zeros((size - tall - half, width), F32)


X1, X2, G, W, OUT = (pl.ds(0, 2), pl.ds(2, 2), pl.ds(4, 2), pl.ds(6, 7), pl.ds(13, 7))


def first_kernel(
    mean_scale, plan, arriving, returning, examples, stash, fwd_routes_t, bwd_routes_t, *rest
):
    hbm, (slow_o, fast_o, ga_o, gb_o), rest = rest[:7], rest[7:11], rest[11:]
    x_s, x2_s, g_s, y_s, d_s, b_s, b2_s, e_s, r_s, r2_s, ga_s, gb_s, *weights, sems = rest
    odd, even, first, last = position()
    slot = plan[0, 0]
    mine = fwd_routes_t.at[0]
    x_wait = fetch(
        [
            ((first,), examples.at[0], mine),
            ((jnp.logical_not(first),), arriving, mine),
        ],
        x_s,
        b_s,
        r_s,
        sems.at[X1],
    )
    copies = fetch_weights(hbm, weights, SOON, sems.at[W])
    x_wait()
    copies.update(fetch_weights(hbm, weights, THEN, sems.at[W]))
    x2_wait = fetch(
        [
            ((last,), arriving, mine),
            ((jnp.logical_not(last),), stash.at[slot], bwd_routes_t.at[slot]),
        ],
        x2_s,
        b2_s,
        r2_s,
        sems.at[X2],
    )
    g_copy = pltpu.make_async_copy(returning, g_s, sems.at[4])
    t_copy = pltpu.make_async_copy(examples.at[0], e_s, sems.at[5])
    pl.when(jnp.logical_not(last))(g_copy.start)
    pl.when(last)(t_copy.start)
    values = primal_of(x_s[...], r_s[...], copies, weights)
    copies["down"].wait()
    y_s[...] = output_of(x_s, values, weights[6])
    outs = sems.at[OUT]
    y_slow = pltpu.make_async_copy(y_s, slow_o, outs.at[0])
    y_fast = pltpu.make_async_copy(y_s, fast_o, outs.at[0])
    d_slow = pltpu.make_async_copy(d_s, slow_o, outs.at[1])
    d_fast = pltpu.make_async_copy(d_s, fast_o, outs.at[1])
    pl.when(odd)(y_slow.start)
    pl.when(even)(y_fast.start)
    x2_wait()

    @pl.when(last)
    def _():
        t_copy.wait()
        g_s[...] = y_s[...] - e_s[...].astype(F32)

    values = primal_of(x2_s[...], r2_s[...], None, weights)
    pl.when(jnp.logical_not(last))(g_copy.wait)
    dx, ga, gb = gradients(x2_s, g_s, values, weights)
    d_s[...] = dx
    pl.when(odd)(d_fast.start)
    pl.when(even)(d_slow.start)
    factor = normalizer(ga, gb, mean_scale)
    ga_s[...] = factor * ga
    gb_s[...] = factor * gb
    tail = [
        pltpu.make_async_copy(ga_s, ga_o, outs.at[2]),
        pltpu.make_async_copy(gb_s, gb_o, outs.at[3]),
    ]
    for copy in tail:
        copy.start()
    for copy in tail:
        copy.wait()

    @pl.when(odd)
    def _():
        y_slow.wait()
        d_fast.wait()

    @pl.when(even)
    def _():
        y_fast.wait()
        d_slow.wait()


def keep(values, saved, saved_o, sems):
    rstd, normed, share, _, low, gate_pre, up_pre = values
    kept = (jnp.broadcast_to(rstd, saved[0].shape), normed, share, low, gate_pre, up_pre)
    moves = []
    for i, value in enumerate(kept):
        saved[i][...] = value
        moves.append(pltpu.make_async_copy(saved[i], saved_o[i], sems.at[i]))
        moves[-1].start()
    for move in moves:
        move.wait()


def recompute_kernel(tick, plan, stash, bwd_routes_t, *rest):
    hbm, saved_o, rest = rest[:7], rest[7:13], rest[13:]
    x_s, b_s, r_s, *rest = rest
    saved, weights, sems = rest[:6], rest[6:13], rest[13]
    slot = plan[0, tick]
    x_wait = fetch(
        [((slot >= 0,), stash.at[slot], bwd_routes_t.at[slot])], x_s, b_s, r_s, sems.at[X1]
    )
    copies = fetch_weights(hbm, weights, SOON, sems.at[W])
    x_wait()
    copies.update(fetch_weights(hbm, weights, ("up",), sems.at[W]))
    keep(primal_of(x_s[...], r_s[...], copies, weights), saved, saved_o, sems.at[OUT])


def backward_of_saved(hbm, weights, saved_cases, saved, g_cases, x_cases, refs, sums_in, sems):
    x_s, g_s, b_s, e_s, ga_s, gb_s = refs
    extra = sems.at[OUT]
    early, late = (2, 4, 5), (0, 1, 3)
    waits = []

    def load(indices):
        for predicates, source in saved_cases:
            moves = [
                pltpu.make_async_copy(source[i], saved[i], extra.at[1 + i]) for i in indices
            ]
            waits.append((predicates, moves))

            @when_all(*predicates)
            def _(moves=moves):
                for move in moves:
                    move.start()

    def settle():
        while waits:
            predicates, moves = waits.pop()

            @when_all(*predicates)
            def _(moves=moves):
                for move in moves:
                    move.wait()

    g_moves = []
    for predicates, source, target in g_cases:
        mine = [pltpu.make_async_copy(source, g_s, sems.at[4])]
        if target is not None:
            mine.append(pltpu.make_async_copy(target, e_s, sems.at[5]))
        g_moves.append((predicates, mine))

        @when_all(*predicates)
        def _(mine=mine):
            for move in mine:
                move.start()

    load(early)
    copies = fetch_weights(hbm, weights, ("down",), sems.at[W])
    settle()
    for predicates, mine in g_moves:

        @when_all(*predicates)
        def _(mine=mine):
            for move in mine:
                move.wait()
            if len(mine) > 1:
                g_s[...] = g_s[...] - e_s[...].astype(F32)

    copies.update(fetch_weights(hbm, weights, ("b", "gate", "up", "router", "a"), sems.at[W]))
    load(late)
    x_wait = fetch(x_cases, x_s, b_s, None, sems.at[X1])
    copies.update(fetch_weights(hbm, weights, ("gain",), sems.at[W]))
    sums = [
        pltpu.make_async_copy(sums_in[0], ga_s, sems.at[2]),
        pltpu.make_async_copy(sums_in[1], gb_s, sems.at[3]),
    ]
    for copy in sums:
        copy.start()

    def values():
        settle()
        x_wait()
        return saved[0][:, 0:1], saved[1][...], saved[3][...]

    result = gradients(x_s, g_s, saved, weights, copies, values)
    for copy in sums:
        copy.wait()
    return result


def second_kernel(
    tick,
    mean_scale,
    plan,
    arrived,
    stash,
    fwd_routes_t,
    ga_in,
    gb_in,
    *rest,
):
    saved_in, rest = rest[:6], rest[6:]
    hbm, (sent, packed, *saved_o), rest = rest[:7], rest[7:15], rest[15:]
    x_s, g_s, y_s, b_s, e_s, r_s, ga_s, gb_s, packed_s, *rest = rest
    saved, weights, sems = rest[:6], rest[6:13], rest[13]
    odd, even, _, last = position()
    outs = sems.at[OUT]
    y_copy = pltpu.make_async_copy(y_s, sent, outs.at[0])

    @pl.when(odd)
    def _():
        x_wait = fetch([((odd,), arrived, fwd_routes_t.at[tick])], x_s, b_s, r_s, sems.at[X1])
        copies = fetch_weights(hbm, weights, SOON, sems.at[W])
        x_wait()
        copies.update(fetch_weights(hbm, weights, THEN, sems.at[W]))
        values = primal_of(x_s[...], r_s[...], copies, weights)
        copies["down"].wait()
        y_s[...] = output_of(x_s, values, weights[6])
        y_copy.start()

        @pl.when(last)
        def _():
            keep(values, saved, saved_o, sems.at[pl.ds(14, 6)])

    @pl.when(even)
    def _():
        dx, ga, gb = backward_of_saved(
            hbm,
            weights,
            [((even,), saved_in)],
            saved,
            [((even,), arrived, None)],
            [((even,), stash.at[plan[0, tick]], None)],
            (x_s, g_s, b_s, e_s, ga_s, gb_s),
            (ga_in, gb_in),
            sems,
        )
        y_s[...] = dx
        y_copy.start()
        factor = normalizer(ga, gb, mean_scale)
        pack(packed_s, ga_s[...] + factor * ga, gb_s[...] + factor * gb)
        move = pltpu.make_async_copy(packed_s, packed, outs.at[1])
        move.start()
        move.wait()

    y_copy.wait()


def third_kernel(
    tick,
    mean_scale,
    plan,
    arrived,
    near,
    output,
    examples,
    stash,
    fwd_routes_t,
    packed_in,
    ga_in,
    gb_in,
    *rest,
):
    saved_in, last_in, rest = rest[:6], rest[6:12], rest[12:]
    hbm, (sent, packed), rest = rest[:7], rest[7:9], rest[9:]
    x_s, g_s, y_s, b_s, e_s, r_s, ga_s, gb_s, packed_s, *rest = rest
    saved, weights, sems = rest[:6], rest[6:13], rest[13]
    odd, even, first, last = position()
    inner = jnp.logical_and(odd, jnp.logical_not(last))
    outs = sems.at[OUT]
    y_copy = pltpu.make_async_copy(y_s, sent, outs.at[0])
    p_copy = pltpu.make_async_copy(packed_s, packed, sems.at[20])

    @pl.when(even)
    def _():
        mine = fwd_routes_t.at[tick]
        x_wait = fetch(
            [
                ((first,), examples.at[tick], mine),
                ((jnp.logical_not(first),), arrived, mine),
            ],
            x_s,
            b_s,
            r_s,
            sems.at[X1],
        )
        copies = fetch_weights(hbm, weights, SOON, sems.at[W])
        x_wait()
        copies.update(fetch_weights(hbm, weights, THEN, sems.at[W]))
        hold = pltpu.make_async_copy(packed_in, packed_s, sems.at[4])
        hold.start()
        values = primal_of(x_s[...], r_s[...], copies, weights)
        copies["down"].wait()
        hold.wait()
        p_copy.start()
        y_s[...] = output_of(x_s, values, weights[6])
        y_copy.start()

    @pl.when(odd)
    def _():
        dx, ga, gb = backward_of_saved(
            hbm,
            weights,
            [((last,), last_in), ((inner,), saved_in)],
            saved,
            [((last,), output, examples.at[tick]), ((inner,), arrived, None)],
            [((last,), near, None), ((inner,), stash.at[plan[0, tick]], None)],
            (x_s, g_s, b_s, e_s, ga_s, gb_s),
            (ga_in, gb_in),
            sems,
        )
        y_s[...] = dx
        y_copy.start()
        factor = normalizer(ga, gb, mean_scale)
        pack(packed_s, ga_s[...] + factor * ga, gb_s[...] + factor * gb)
        p_copy.start()

    y_copy.wait()
    p_copy.wait()


def sum_kernel(parts, total):
    total[...] = jnp.sum(parts[...], axis=0).reshape(total.shape)


def final_kernel(tall, half, pieces, parts, slow, fast, ga, gb, acts_o, grads_o, slow_s, fast_s, sems):
    odd, even, _, _ = position()
    rows = slow.shape[0] // pieces
    moves = []
    for source, stage, low, high in (
        (slow, slow_s, acts_o, grads_o),
        (fast, fast_s, grads_o, acts_o),
    ):
        for i in range(pieces):
            at = pl.ds(i * rows, rows)
            k = 2 * len(moves)
            move_in = pltpu.make_async_copy(source.at[at], stage.at[at], sems.at[k])
            move_even = pltpu.make_async_copy(stage.at[at], low.at[at], sems.at[k + 1])
            move_odd = pltpu.make_async_copy(stage.at[at], high.at[at], sems.at[k + 1])
            moves.append((move_in, move_even, move_odd))
    for move_in, _, _ in moves:
        move_in.start()
    for move_in, move_even, move_odd in moves:
        move_in.wait()
        pl.when(even)(move_even.start)
        pl.when(odd)(move_odd.start)
    total = jnp.sum(parts[...], axis=0)
    ga[...] = total[:tall]
    rank = gb.shape[2]
    for side in range(2):
        for part in range(2):
            lane = part * tall + side * rank
            gb[side, part * half : (part + 1) * half, :] = total[
                tall : tall + half, lane : lane + rank
            ]
    for _, move_even, move_odd in moves:
        pl.when(even)(move_even.wait)
        pl.when(odd)(move_odd.wait)


def swaps(first, count):
    pairs = []
    for s in range(first, count - 1, 2):
        pairs += [(s, s + 1), (s + 1, s)]
    return pairs


def shards(
    y_size,
    examples,
    arriving,
    returning,
    stash,
    plan,
    forward_expert_routes,
    backward_expert_routes,
    input_norm_gain,
    router,
    frozen_gate_weight,
    frozen_up_weight,
    frozen_down_weight,
    down_factors,
    up_factors,
):
    replicas = lax.axis_size("dp")
    z_size = replicas // y_size
    ticks, tokens, width = examples.shape
    mean_scale = 1.0 / (ticks * replicas)
    gain, router, gate, up, down = (
        input_norm_gain,
        router[0],
        frozen_gate_weight[0],
        frozen_up_weight[0],
        frozen_down_weight[0],
    )
    a_t = down_factors[0].T
    b = up_factors[0]
    stash = stash[0]
    fwd_routes_t = jnp.swapaxes(forward_expert_routes[0], 1, 2)
    bwd_routes_t = jnp.swapaxes(backward_expert_routes[0], 1, 2)
    topk = fwd_routes_t.shape[1]
    hidden_units = gate.shape[1]
    columns = a_t.shape[0]
    weights = (gain, router, a_t, gate, up, b, down)
    scratch = [pltpu.VMEM(w.shape, w.dtype) for w in weights]
    x_scratch = pltpu.VMEM((tokens, width), F32)
    b_scratch = pltpu.VMEM((tokens, width), BF16)
    r_scratch = pltpu.VMEM((topk, tokens), jnp.int32)
    semaphores = pltpu.SemaphoreType.DMA((21,))
    sections = lax.axis_size("section")
    near = swaps(0, sections)
    far = swaps(1, sections)
    rows_each = hidden_units // replicas
    size = columns + -(-(rows_each // 2) // 8) * 8
    share_width = width // replicas
    activation = jax.ShapeDtypeStruct((tokens, width), F32)
    sums_shape = (
        jax.ShapeDtypeStruct((columns, width), F32),
        jax.ShapeDtypeStruct((columns, hidden_units), F32),
    )
    packed_shape = jax.ShapeDtypeStruct((y_size, z_size * size, share_width), F32)
    saved_shape = (
        jax.ShapeDtypeStruct((tokens, 128), F32),
        jax.ShapeDtypeStruct((tokens, width), BF16),
        jax.ShapeDtypeStruct((tokens, router.shape[1]), F32),
        jax.ShapeDtypeStruct((tokens, columns), BF16),
        jax.ShapeDtypeStruct((tokens, hidden_units), F32),
        jax.ShapeDtypeStruct((tokens, hidden_units), F32),
    )

    def rooms(shapes):
        return [pltpu.VMEM(shape.shape, shape.dtype) for shape in shapes]

    primal_flops = 2 * tokens * width * (router.shape[1] + columns + 2 * hidden_units)
    down_flops = 2 * tokens * width * hidden_units
    weight_bytes = sum(w.size * w.dtype.itemsize for w in weights)

    def kernel(body, flops, outs, rooms, operands):
        return pl.pallas_call(
            body,
            out_shape=outs,
            in_specs=[SMEM] + [ANY] * (len(operands) - 1),
            out_specs=(ANY,) * len(outs),
            scratch_shapes=[*rooms, *scratch, semaphores],
            compiler_params=pltpu.CompilerParams(vmem_limit_bytes=67043328),
            cost_estimate=pl.CostEstimate(
                flops=flops, bytes_accessed=weight_bytes + 8 * tokens * width, transcendentals=0
            ),
        )(*operands)

    slow, fast, *sums = kernel(
        functools.partial(first_kernel, mean_scale),
        3 * primal_flops + 2 * down_flops,
        (activation, activation, *sums_shape),
        [x_scratch] * 5 + [b_scratch] * 3 + [r_scratch] * 2 + rooms(sums_shape),
        (plan, arriving[0], returning[0], examples, stash, fwd_routes_t, bwd_routes_t, *weights),
    )
    slow_0 = lax.ppermute(slow, "section", far)
    fast_0 = lax.ppermute(fast, "section", near)
    saved = kernel(
        functools.partial(recompute_kernel, 1),
        primal_flops,
        saved_shape,
        [x_scratch, b_scratch, r_scratch] + rooms(saved_shape),
        (plan, stash, bwd_routes_t, *weights),
    )
    ahead, packed, *last_saved = kernel(
        functools.partial(second_kernel, 1, mean_scale),
        primal_flops + down_flops,
        (activation, packed_shape, *saved_shape),
        [x_scratch] * 3
        + [b_scratch] * 2
        + [r_scratch]
        + rooms((*sums_shape, packed_shape, *saved_shape)),
        (plan, fast_0, stash, fwd_routes_t, *sums, *saved, *weights),
    )
    slow_1 = lax.ppermute(ahead, "section", far)
    sent, packed = kernel(
        functools.partial(third_kernel, 1, mean_scale),
        primal_flops + down_flops,
        (activation, packed_shape),
        [x_scratch] * 3
        + [b_scratch] * 2
        + [r_scratch]
        + rooms((*sums_shape, packed_shape, *saved_shape)),
        (
            plan,
            slow_0,
            fast_0,
            ahead,
            examples,
            stash,
            fwd_routes_t,
            packed,
            *sums,
            *saved,
            *last_saved,
            *weights,
        ),
    )
    fast_1 = lax.ppermute(sent, "section", near)
    y_groups = [[z * y_size + y for y in range(y_size)] for z in range(z_size)]
    z_groups = [[z * y_size + y for z in range(z_size)] for y in range(y_size)]
    parts = lax.all_to_all(packed, "dp", 0, 0, axis_index_groups=y_groups, tiled=True)
    parts = pl.pallas_call(
        sum_kernel,
        out_shape=jax.ShapeDtypeStruct((z_size, size, share_width), F32),
        in_specs=[VMEM],
        out_specs=VMEM,
        compiler_params=pltpu.CompilerParams(vmem_limit_bytes=8 << 20),
        name="sum_y",
    )(parts)
    parts = lax.all_to_all(parts, "dp", 0, 0, axis_index_groups=z_groups, tiled=True)
    pieces = 4
    share_a, share_b, next_acts, next_grads = pl.pallas_call(
        functools.partial(final_kernel, columns, rows_each // 2, pieces),
        out_shape=(
            jax.ShapeDtypeStruct((columns, share_width), F32),
            jax.ShapeDtypeStruct((2, rows_each, columns // 2), F32),
            activation,
            activation,
        ),
        in_specs=[VMEM, ANY, ANY],
        out_specs=(VMEM, VMEM, ANY, ANY),
        scratch_shapes=[x_scratch, x_scratch, pltpu.SemaphoreType.DMA((4 * pieces,))],
        compiler_params=pltpu.CompilerParams(vmem_limit_bytes=8 << 20),
        name="sum_dp",
    )(parts, slow_1, fast_1)
    return (
        next_acts[None],
        next_grads[None],
        share_a.T[None],
        jnp.swapaxes(share_b, 1, 2)[None],
    )


def solution(mesh):
    in_specs = (
        P(None, "dp", None),
        P("section", "dp", None),
        P("section", "dp", None),
        P("section", None, "dp", None),
        P("section", None),
        P("section", None, "dp", None),
        P("section", None, "dp", None),
        P("section", None),
        P("section", None, None),
        P("section", None, None),
        P("section", None, None),
        P("section", None, None),
        P("section", None, None),
        P("section", None, None, None),
    )
    out_specs = (
        P("section", "dp", None),
        P("section", "dp", None),
        P("section", "dp", None),
        P("section", None, None, "dp"),
    )

    def body(*args):
        return shards(4, *args)

    return jax.shard_map(
        body, mesh=mesh, in_specs=in_specs, out_specs=out_specs, check_vma=False
    )
```

```python
import functools

import jax
import jax.numpy as jnp
from jax import lax
from jax.experimental import pallas as pl
from jax.experimental.pallas import tpu as pltpu
from jax.sharding import PartitionSpec as P


SCALE = 2.0
EPS = 1e-06
F32 = jnp.float32
BF16 = jnp.bfloat16
ANY = pl.BlockSpec(memory_space=pl.ANY)
SMEM = pl.BlockSpec(memory_space=pltpu.SMEM)
VMEM = pl.BlockSpec(memory_space=pltpu.VMEM)


def nn(a, b):
    return jnp.dot(a, b, preferred_element_type=F32)


def nt(a, b):
    return lax.dot_general(a, b, (((1,), (1,)), ((), ())), preferred_element_type=F32)


def primal(x, routes_t, gain, copies, router, a_t, gate, up, factors):
    def ready(name):
        if copies is not None:
            copies[name].wait()

    rstd = lax.rsqrt(jnp.mean(x * x, axis=-1, keepdims=True) + EPS)
    normed = (x * rstd * gain).astype(BF16)
    ready("router")
    logits = nn(normed, router[...])
    experts = logits.shape[1]
    expert = lax.broadcasted_iota(jnp.int32, (experts, routes_t.shape[1]), 0)
    named = jnp.zeros(expert.shape, F32)
    for k in range(routes_t.shape[0]):
        named = jnp.where(routes_t[k : k + 1, :] == expert, 1.0, named)
    scores = jnp.where(named.T > 0.5, jnp.exp(logits), 0.0)
    share = scores / jnp.sum(scores, axis=-1, keepdims=True)
    weight = share[:, 0:1]
    ready("a")
    low = nt(normed, a_t[...]).astype(BF16)
    rank = low.shape[1] // 2
    ready("b")
    ready("gate")
    gate_pre = nn(normed, gate[...]) + SCALE * nn(low[:, :rank], factors[0])
    ready("up")
    up_pre = nn(normed, up[...]) + SCALE * nn(low[:, rank:], factors[1])
    return rstd, normed, share, weight, low, gate_pre, up_pre


def when_all(*predicates):
    both = predicates[0]
    for predicate in predicates[1:]:
        both = jnp.logical_and(both, predicate)
    return pl.when(both)


def position():
    section = lax.axis_index("section")
    odd = lax.rem(section, 2) == 1
    return (
        odd,
        jnp.logical_not(odd),
        section == 0,
        section == lax.axis_size("section") - 1,
    )


def fetch(cases, x_s, b_s, r_s, sems):
    moves = []
    for predicates, source, routes in cases:
        narrow = source.dtype == BF16
        mine = [pltpu.make_async_copy(source, b_s if narrow else x_s, sems.at[0])]
        if routes is not None:
            mine.append(pltpu.make_async_copy(routes, r_s, sems.at[1]))
        moves.append((predicates, narrow, mine))

        @when_all(*predicates)
        def _(mine=mine):
            for copy in mine:
                copy.start()

    def wait():
        for predicates, narrow, mine in moves:

            @when_all(*predicates)
            def _(narrow=narrow, mine=mine):
                for copy in mine:
                    copy.wait()
                if narrow:
                    x_s[...] = b_s[...].astype(F32)

    return wait


NAMES = ("gain", "router", "a", "gate", "up", "b", "down")


def fetch_weights(hbm, weights, order, sems):
    copies = {}
    for name in order:
        i = NAMES.index(name)
        copies[name] = pltpu.make_async_copy(hbm[i], weights[i], sems.at[i])
        copies[name].start()
    return copies


def primal_of(x, routes, copies, weights):
    gain_s, router, a_t, gate, up, factors = weights[:6]
    if copies is not None:
        copies["gain"].wait()
    return primal(x, routes, gain_s[...], copies, router, a_t, gate, up, factors)


def output_of(x_s, values, down):
    _, _, _, weight, _, gate_pre, up_pre = values
    hidden = (gate_pre * jax.nn.sigmoid(gate_pre) * up_pre).astype(BF16)
    return x_s[...] + weight * nn(hidden, down[...])


def gradients(x_s, g_s, saved, weights, copies=None, late=None):
    def ready(*names):
        if copies is not None:
            for name in names:
                copies[name].wait()

    gain_s, router, a_t, gate, up, factors, down = weights
    if late is None:
        rstd, normed, share, weight, low, gate_pre, up_pre = saved
    else:
        share, gate_pre, up_pre = (saved[i][...] for i in (2, 4, 5))
        weight = share[:, 0:1]
    sig = jax.nn.sigmoid(gate_pre)
    silu = gate_pre * sig
    hidden = (silu * up_pre).astype(BF16)
    ready("down")
    back = nt(g_s[...].astype(BF16), down[...])
    d_weight = jnp.sum(hidden.astype(F32) * back, axis=-1, keepdims=True)
    lead = (lax.broadcasted_iota(jnp.int32, share.shape, 1) == 0).astype(F32)
    d_logits = ((d_weight * weight) * (lead - share)).astype(BF16)
    d_hidden = (weight * back).astype(BF16).astype(F32)
    d_gate = (d_hidden * up_pre * (sig * (1.0 + gate_pre * (1.0 - sig)))).astype(BF16)
    d_up = (d_hidden * silu).astype(BF16)
    ready("b", "gate", "up", "router", "a", "gain")
    if late is not None:
        rstd, normed, low = late()
    d_low_f = SCALE * jnp.concatenate([nt(d_gate, factors[0]), nt(d_up, factors[1])], axis=1)
    d_normed = (
        nt(d_gate, gate[...])
        + nt(d_up, up[...])
        + nt(d_logits, router[...])
        + nn(d_low_f.astype(BF16), a_t[...])
    )
    scaled = d_normed * gain_s[...]
    x = x_s[...]
    along = jnp.mean(scaled * x, axis=-1, keepdims=True) * (rstd * rstd)
    dx = g_s[...] + rstd * (scaled - x * along)
    rank = low.shape[1] // 2
    ga = nn(d_low_f.T.astype(BF16), normed)
    low_t = low.astype(F32).T.astype(BF16)
    gb = SCALE * jnp.concatenate([nn(low_t[:rank], d_gate), nn(low_t[rank:], d_up)], axis=0)
    return dx, ga, gb


def normalizer(ga, gb, mean_scale):
    square = (jnp.sum(ga * ga) + jnp.sum(gb * gb)) / (ga.size + gb.size)
    return lax.rsqrt(square + EPS) * mean_scale


def pack(packed, ga, gb):
    gb_t = gb.T
    ys, _, width = packed.shape
    zs = ga.shape[1] // (ys * width)
    size = packed.shape[1] // zs
    rows = gb_t.shape[0] // (ys * zs)
    tall = ga.shape[0]
    half = rows // 2
    for y in range(ys):
        for z in range(zs):
            p = z * ys + y
            at = z * size
            packed[y, at : at + tall, :] = ga[:, p * width : (p + 1) * width]
            at += tall
            packed[y, at : at + half, :tall] = gb_t[p * rows : p * rows + half]
            packed[y, at : at + half, tall:] = gb_t[p * rows + half : (p + 1) * rows]
            packed[y, at + half : (z + 1) * size, :] = jnp.zeros((size - tall - half, width), F32)


FIRST_ORDER = ("gain", "router", "a", "b", "gate", "up", "down")
X1, X2, G, W, OUT = (pl.ds(0, 2), pl.ds(2, 2), pl.ds(4, 2), pl.ds(6, 7), pl.ds(13, 7))


def first_kernel(
    mean_scale, plan, arriving, returning, examples, stash, fwd_routes_t, bwd_routes_t, *rest
):
    hbm, (slow_o, fast_o, ga_o, gb_o), rest = rest[:7], rest[7:11], rest[11:]
    x_s, x2_s, g_s, y_s, d_s, b_s, b2_s, e_s, r_s, r2_s, ga_s, gb_s, *weights, sems = rest
    odd, even, first, last = position()
    slot = plan[0, 0]
    mine = fwd_routes_t.at[0]
    x_wait = fetch(
        [
            ((first,), examples.at[0], mine),
            ((jnp.logical_not(first),), arriving, mine),
        ],
        x_s,
        b_s,
        r_s,
        sems.at[X1],
    )
    copies = fetch_weights(hbm, weights, FIRST_ORDER, sems.at[W])
    x2_wait = fetch(
        [
            ((last,), arriving, mine),
            ((jnp.logical_not(last),), stash.at[slot], bwd_routes_t.at[slot]),
        ],
        x2_s,
        b2_s,
        r2_s,
        sems.at[X2],
    )
    g_copy = pltpu.make_async_copy(returning, g_s, sems.at[4])
    t_copy = pltpu.make_async_copy(examples.at[0], e_s, sems.at[5])
    pl.when(jnp.logical_not(last))(g_copy.start)
    pl.when(last)(t_copy.start)
    x_wait()
    values = primal_of(x_s[...], r_s[...], copies, weights)
    copies["down"].wait()
    y_s[...] = output_of(x_s, values, weights[6])
    outs = sems.at[OUT]
    y_slow = pltpu.make_async_copy(y_s, slow_o, outs.at[0])
    y_fast = pltpu.make_async_copy(y_s, fast_o, outs.at[0])
    d_slow = pltpu.make_async_copy(d_s, slow_o, outs.at[1])
    d_fast = pltpu.make_async_copy(d_s, fast_o, outs.at[1])
    pl.when(odd)(y_slow.start)
    pl.when(even)(y_fast.start)
    x2_wait()

    @pl.when(last)
    def _():
        t_copy.wait()
        g_s[...] = y_s[...] - e_s[...].astype(F32)

    values = primal_of(x2_s[...], r2_s[...], None, weights)
    pl.when(jnp.logical_not(last))(g_copy.wait)
    dx, ga, gb = gradients(x2_s, g_s, values, weights)
    d_s[...] = dx
    pl.when(odd)(d_fast.start)
    pl.when(even)(d_slow.start)
    factor = normalizer(ga, gb, mean_scale)
    ga_s[...] = factor * ga
    gb_s[...] = factor * gb
    tail = [
        pltpu.make_async_copy(ga_s, ga_o, outs.at[2]),
        pltpu.make_async_copy(gb_s, gb_o, outs.at[3]),
    ]
    for copy in tail:
        copy.start()
    for copy in tail:
        copy.wait()

    @pl.when(odd)
    def _():
        y_slow.wait()
        d_fast.wait()

    @pl.when(even)
    def _():
        y_fast.wait()
        d_slow.wait()


def fill_kernel(gain, token, gain_s, sem):
    copy = pltpu.make_async_copy(gain, gain_s, sem)
    copy.start()
    copy.wait()
    token[...] = jnp.broadcast_to(gain_s[:, :128], token.shape)


def second_kernel(
    tick, mean_scale, plan, arrived, after, stash, fwd_routes_t, bwd_routes_t, ga_in, gb_in, *rest
):
    hbm, (sent, packed, *saved_o), rest = rest[:7], rest[7:15], rest[15:]
    x_s, x2_s, y_s, b_s, b2_s, r_s, r2_s, ga_s, gb_s, packed_s, *rest = rest
    saved, weights, sems = rest[:6], rest[6:13], rest[13]
    odd, even, _, last = position()
    slot = plan[0, tick]
    mine = fwd_routes_t.at[tick]
    stored = (stash.at[slot], bwd_routes_t.at[slot])
    inner = jnp.logical_and(odd, jnp.logical_not(last))
    x_wait = fetch([((odd,), arrived, mine), ((even,), *stored)], x_s, b_s, r_s, sems.at[X1])
    copies = fetch_weights(hbm, weights, FIRST_ORDER, sems.at[W])
    x2_wait = fetch(
        [((last,), arrived, mine), ((inner,), *stored)], x2_s, b2_s, r2_s, sems.at[X2]
    )
    g_copies = [
        pltpu.make_async_copy(arrived, x2_s, sems.at[4]),
        pltpu.make_async_copy(ga_in, ga_s, sems.at[5]),
        pltpu.make_async_copy(gb_in, gb_s, sems.at[20]),
    ]

    @pl.when(even)
    def _():
        for copy in g_copies:
            copy.start()

    x_wait()
    values = primal_of(x_s[...], r_s[...], copies, weights)
    copies["down"].wait()
    outs = sems.at[OUT]
    y_copy = pltpu.make_async_copy(y_s, sent, outs.at[0])

    @pl.when(odd)
    def _():
        y_s[...] = output_of(x_s, values, weights[6])
        y_copy.start()
        x2_wait()
        rstd, normed, share, _, low, gate_pre, up_pre = primal_of(
            x2_s[...], r2_s[...], None, weights
        )
        kept = (jnp.broadcast_to(rstd, saved[0].shape), normed, share, low, gate_pre, up_pre)
        moves = []
        for i, value in enumerate(kept):
            saved[i][...] = value
            moves.append(pltpu.make_async_copy(saved[i], saved_o[i], outs.at[1 + i]))
            moves[-1].start()
        for move in moves:
            move.wait()

    @pl.when(even)
    def _():
        for copy in g_copies:
            copy.wait()
        dx, ga, gb = gradients(x_s, x2_s, values, weights)
        y_s[...] = dx
        y_copy.start()
        factor = normalizer(ga, gb, mean_scale)
        pack(packed_s, ga_s[...] + factor * ga, gb_s[...] + factor * gb)
        move = pltpu.make_async_copy(packed_s, packed, outs.at[1])
        move.start()
        move.wait()

    y_copy.wait()


def third_kernel(
    tick,
    mean_scale,
    plan,
    arrived,
    near,
    output,
    examples,
    stash,
    fwd_routes_t,
    packed_in,
    ga_in,
    gb_in,
    *rest,
):
    saved_in, rest = rest[:6], rest[6:]
    hbm, (sent, packed), rest = rest[:7], rest[7:9], rest[9:]
    x_s, g_s, y_s, b_s, e_s, r_s, ga_s, gb_s, packed_s, *rest = rest
    saved, weights, sems = rest[:6], rest[6:13], rest[13]
    odd, even, first, last = position()
    inner = jnp.logical_and(odd, jnp.logical_not(last))
    outs = sems.at[OUT]
    y_copy = pltpu.make_async_copy(y_s, sent, outs.at[0])
    p_copy = pltpu.make_async_copy(packed_s, packed, sems.at[20])

    @pl.when(even)
    def _():
        mine = fwd_routes_t.at[tick]
        x_wait = fetch(
            [
                ((first,), examples.at[tick], mine),
                ((jnp.logical_not(first),), arrived, mine),
            ],
            x_s,
            b_s,
            r_s,
            sems.at[X1],
        )
        copies = fetch_weights(hbm, weights, FIRST_ORDER, sems.at[W])
        keep = pltpu.make_async_copy(packed_in, packed_s, sems.at[4])
        keep.start()
        x_wait()
        values = primal_of(x_s[...], r_s[...], copies, weights)
        copies["down"].wait()
        keep.wait()
        p_copy.start()
        y_s[...] = output_of(x_s, values, weights[6])
        y_copy.start()

    @pl.when(odd)
    def _():
        g_copy = pltpu.make_async_copy(arrived, g_s, sems.at[4])
        o_copy = pltpu.make_async_copy(output, g_s, sems.at[4])
        t_copy = pltpu.make_async_copy(examples.at[tick], e_s, sems.at[5])
        pl.when(inner)(g_copy.start)

        @pl.when(last)
        def _():
            o_copy.start()
            t_copy.start()

        moves = [pltpu.make_async_copy(saved_in[i], saved[i], outs.at[1 + i]) for i in range(6)]
        for i in (2, 4, 5):
            moves[i].start()
        copies = fetch_weights(hbm, weights, ("down", "gate", "up", "b", "router", "a"), sems.at[W])
        for i in (0, 1, 3):
            moves[i].start()
        x_wait = fetch(
            [((last,), near, None), ((inner,), stash.at[plan[0, tick]], None)],
            x_s,
            b_s,
            None,
            sems.at[X1],
        )
        copies.update(fetch_weights(hbm, weights, ("gain",), sems.at[W]))
        sums = [
            pltpu.make_async_copy(ga_in, ga_s, sems.at[2]),
            pltpu.make_async_copy(gb_in, gb_s, sems.at[3]),
        ]
        for copy in sums:
            copy.start()
        for i in (2, 4, 5):
            moves[i].wait()
        pl.when(inner)(g_copy.wait)

        @pl.when(last)
        def _():
            o_copy.wait()
            t_copy.wait()
            g_s[...] = g_s[...] - e_s[...].astype(F32)

        def late():
            for i in (0, 1, 3):
                moves[i].wait()
            x_wait()
            return saved[0][:, 0:1], saved[1][...], saved[3][...]

        dx, ga, gb = gradients(x_s, g_s, saved, weights, copies, late)
        y_s[...] = dx
        y_copy.start()
        factor = normalizer(ga, gb, mean_scale)
        for copy in sums:
            copy.wait()
        pack(packed_s, ga_s[...] + factor * ga, gb_s[...] + factor * gb)
        p_copy.start()

    y_copy.wait()
    p_copy.wait()


def sum_kernel(parts, total):
    total[...] = jnp.sum(parts[...], axis=0).reshape(total.shape)


def final_kernel(tall, half, pieces, parts, slow, fast, ga, gb, acts_o, grads_o, slow_s, fast_s, sems):
    odd, even, _, _ = position()
    rows = slow.shape[0] // pieces
    moves = []
    for source, stage, low, high in (
        (slow, slow_s, acts_o, grads_o),
        (fast, fast_s, grads_o, acts_o),
    ):
        for i in range(pieces):
            at = pl.ds(i * rows, rows)
            k = 2 * len(moves)
            move_in = pltpu.make_async_copy(source.at[at], stage.at[at], sems.at[k])
            move_even = pltpu.make_async_copy(stage.at[at], low.at[at], sems.at[k + 1])
            move_odd = pltpu.make_async_copy(stage.at[at], high.at[at], sems.at[k + 1])
            moves.append((move_in, move_even, move_odd))
    for move_in, _, _ in moves:
        move_in.start()
    for move_in, move_even, move_odd in moves:
        move_in.wait()
        pl.when(even)(move_even.start)
        pl.when(odd)(move_odd.start)
    total = jnp.sum(parts[...], axis=0)
    ga[...] = total[:tall]
    rank = gb.shape[2]
    for side in range(2):
        for part in range(2):
            lane = part * tall + side * rank
            gb[side, part * half : (part + 1) * half, :] = total[
                tall : tall + half, lane : lane + rank
            ]
    for _, move_even, move_odd in moves:
        pl.when(even)(move_even.wait)
        pl.when(odd)(move_odd.wait)


def swaps(first, count):
    pairs = []
    for s in range(first, count - 1, 2):
        pairs += [(s, s + 1), (s + 1, s)]
    return pairs


def shards(
    y_size,
    examples,
    arriving,
    returning,
    stash,
    plan,
    forward_expert_routes,
    backward_expert_routes,
    input_norm_gain,
    router,
    frozen_gate_weight,
    frozen_up_weight,
    frozen_down_weight,
    down_factors,
    up_factors,
):
    replicas = lax.axis_size("dp")
    z_size = replicas // y_size
    ticks, tokens, width = examples.shape
    mean_scale = 1.0 / (ticks * replicas)
    gain, router, gate, up, down = (
        input_norm_gain,
        router[0],
        frozen_gate_weight[0],
        frozen_up_weight[0],
        frozen_down_weight[0],
    )
    a_t = down_factors[0].T
    b = up_factors[0]
    stash = stash[0]
    fwd_routes_t = jnp.swapaxes(forward_expert_routes[0], 1, 2)
    bwd_routes_t = jnp.swapaxes(backward_expert_routes[0], 1, 2)
    topk = fwd_routes_t.shape[1]
    hidden_units = gate.shape[1]
    columns = a_t.shape[0]
    weights = (gain, router, a_t, gate, up, b, down)
    scratch = [pltpu.VMEM(w.shape, w.dtype) for w in weights]
    x_scratch = pltpu.VMEM((tokens, width), F32)
    b_scratch = pltpu.VMEM((tokens, width), BF16)
    r_scratch = pltpu.VMEM((topk, tokens), jnp.int32)
    semaphores = pltpu.SemaphoreType.DMA((21,))
    sections = lax.axis_size("section")
    near = swaps(0, sections)
    far = swaps(1, sections)
    rows_each = hidden_units // replicas
    size = columns + -(-(rows_each // 2) // 8) * 8
    share_width = width // replicas
    activation = jax.ShapeDtypeStruct((tokens, width), F32)
    sums_shape = (
        jax.ShapeDtypeStruct((columns, width), F32),
        jax.ShapeDtypeStruct((columns, hidden_units), F32),
    )
    packed_shape = jax.ShapeDtypeStruct((y_size, z_size * size, share_width), F32)
    saved_shape = (
        jax.ShapeDtypeStruct((tokens, 128), F32),
        jax.ShapeDtypeStruct((tokens, width), BF16),
        jax.ShapeDtypeStruct((tokens, router.shape[1]), F32),
        jax.ShapeDtypeStruct((tokens, columns), BF16),
        jax.ShapeDtypeStruct((tokens, hidden_units), F32),
        jax.ShapeDtypeStruct((tokens, hidden_units), F32),
    )

    def rooms(shapes):
        return [pltpu.VMEM(shape.shape, shape.dtype) for shape in shapes]

    primal_flops = 2 * tokens * width * (router.shape[1] + columns + 2 * hidden_units)
    down_flops = 2 * tokens * width * hidden_units
    weight_bytes = sum(w.size * w.dtype.itemsize for w in weights)

    def kernel(body, flops, outs, rooms, operands):
        return pl.pallas_call(
            body,
            out_shape=outs,
            in_specs=[SMEM] + [ANY] * (len(operands) - 1),
            out_specs=(ANY,) * len(outs),
            scratch_shapes=[*rooms, *scratch, semaphores],
            compiler_params=pltpu.CompilerParams(vmem_limit_bytes=67043328),
            cost_estimate=pl.CostEstimate(
                flops=flops, bytes_accessed=weight_bytes + 8 * tokens * width, transcendentals=0
            ),
        )(*operands)

    slow, fast, *sums = kernel(
        functools.partial(first_kernel, mean_scale),
        3 * primal_flops + 2 * down_flops,
        (activation, activation, *sums_shape),
        [x_scratch] * 5 + [b_scratch] * 3 + [r_scratch] * 2 + rooms(sums_shape),
        (plan, arriving[0], returning[0], examples, stash, fwd_routes_t, bwd_routes_t, *weights),
    )
    slow_0 = lax.ppermute(slow, "section", far)
    fast_0 = lax.ppermute(fast, "section", near)
    whole = pltpu.CompilerParams(vmem_limit_bytes=67043328)
    token = pl.pallas_call(
        fill_kernel,
        out_shape=jax.ShapeDtypeStruct((8, 128), F32),
        in_specs=[ANY],
        out_specs=VMEM,
        scratch_shapes=[pltpu.VMEM(gain.shape, F32), pltpu.SemaphoreType.DMA],
        compiler_params=whole,
        name="fill",
    )(gain)
    ahead, packed, *saved = kernel(
        functools.partial(second_kernel, 1, mean_scale),
        2 * primal_flops + down_flops,
        (activation, packed_shape, *saved_shape),
        [x_scratch] * 3
        + [b_scratch] * 2
        + [r_scratch] * 2
        + rooms((*sums_shape, packed_shape, *saved_shape)),
        (plan, fast_0, token, stash, fwd_routes_t, bwd_routes_t, *sums, *weights),
    )
    slow_1 = lax.ppermute(ahead, "section", far)
    sent, packed = kernel(
        functools.partial(third_kernel, 1, mean_scale),
        primal_flops + down_flops,
        (activation, packed_shape),
        [x_scratch] * 3
        + [b_scratch] * 2
        + [r_scratch]
        + rooms((*sums_shape, packed_shape, *saved_shape)),
        (plan, slow_0, fast_0, ahead, examples, stash, fwd_routes_t, packed, *sums, *saved, *weights),
    )
    y_groups = [[z * y_size + y for y in range(y_size)] for z in range(z_size)]
    z_groups = [[z * y_size + y for z in range(z_size)] for y in range(y_size)]
    parts = lax.all_to_all(packed, "dp", 0, 0, axis_index_groups=y_groups, tiled=True)
    fast_1 = lax.ppermute(sent, "section", near)
    parts = pl.pallas_call(
        sum_kernel,
        out_shape=jax.ShapeDtypeStruct((z_size, size, share_width), F32),
        in_specs=[VMEM],
        out_specs=VMEM,
        compiler_params=pltpu.CompilerParams(vmem_limit_bytes=8 << 20),
        name="sum_y",
    )(parts)
    parts, slow_1 = lax.optimization_barrier((parts, slow_1))
    parts = lax.all_to_all(parts, "dp", 0, 0, axis_index_groups=z_groups, tiled=True)
    pieces = 4
    share_a, share_b, next_acts, next_grads = pl.pallas_call(
        functools.partial(final_kernel, columns, rows_each // 2, pieces),
        out_shape=(
            jax.ShapeDtypeStruct((columns, share_width), F32),
            jax.ShapeDtypeStruct((2, rows_each, columns // 2), F32),
            activation,
            activation,
        ),
        in_specs=[VMEM, ANY, ANY],
        out_specs=(VMEM, VMEM, ANY, ANY),
        scratch_shapes=[x_scratch, x_scratch, pltpu.SemaphoreType.DMA((4 * pieces,))],
        compiler_params=pltpu.CompilerParams(vmem_limit_bytes=8 << 20),
        name="sum_dp",
    )(parts, slow_1, fast_1)
    return (
        next_acts[None],
        next_grads[None],
        share_a.T[None],
        jnp.swapaxes(share_b, 1, 2)[None],
    )


def solution(mesh):
    in_specs = (
        P(None, "dp", None),
        P("section", "dp", None),
        P("section", "dp", None),
        P("section", None, "dp", None),
        P("section", None),
        P("section", None, "dp", None),
        P("section", None, "dp", None),
        P("section", None),
        P("section", None, None),
        P("section", None, None),
        P("section", None, None),
        P("section", None, None),
        P("section", None, None),
        P("section", None, None, None),
    )
    out_specs = (
        P("section", "dp", None),
        P("section", "dp", None),
        P("section", "dp", None),
        P("section", None, None, "dp"),
    )

    def body(*args):
        return shards(4, *args)

    return jax.shard_map(
        body, mesh=mesh, in_specs=in_specs, out_specs=out_specs, check_vma=False
    )
```

```python
import functools

import jax
import jax.numpy as jnp
from jax import lax
from jax.experimental import pallas as pl
from jax.experimental.pallas import tpu as pltpu
from jax.sharding import PartitionSpec as P


SCALE = 2.0
EPS = 1e-06
F32 = jnp.float32
BF16 = jnp.bfloat16
ANY = pl.BlockSpec(memory_space=pl.ANY)
SMEM = pl.BlockSpec(memory_space=pltpu.SMEM)
VMEM = pl.BlockSpec(memory_space=pltpu.VMEM)


def nn(a, b):
    return jnp.dot(a, b, preferred_element_type=F32)


def nt(a, b):
    return lax.dot_general(a, b, (((1,), (1,)), ((), ())), preferred_element_type=F32)


def primal(x, routes_t, gain, copies, router, a_t, gate, up, factors):
    def ready(name):
        if copies is not None:
            copies[name].wait()

    rstd = lax.rsqrt(jnp.mean(x * x, axis=-1, keepdims=True) + EPS)
    normed = (x * rstd * gain).astype(BF16)
    ready("router")
    logits = nn(normed, router[...])
    experts = logits.shape[1]
    expert = lax.broadcasted_iota(jnp.int32, (experts, routes_t.shape[1]), 0)
    named = jnp.zeros(expert.shape, F32)
    for k in range(routes_t.shape[0]):
        named = jnp.where(routes_t[k : k + 1, :] == expert, 1.0, named)
    scores = jnp.where(named.T > 0.5, jnp.exp(logits), 0.0)
    share = scores / jnp.sum(scores, axis=-1, keepdims=True)
    weight = share[:, 0:1]
    ready("a")
    low = nt(normed, a_t[...]).astype(BF16)
    rank = low.shape[1] // 2
    ready("b")
    ready("gate")
    gate_pre = nn(normed, gate[...]) + SCALE * nn(low[:, :rank], factors[0])
    ready("up")
    up_pre = nn(normed, up[...]) + SCALE * nn(low[:, rank:], factors[1])
    return rstd, normed, share, weight, low, gate_pre, up_pre


def when_all(*predicates):
    both = predicates[0]
    for predicate in predicates[1:]:
        both = jnp.logical_and(both, predicate)
    return pl.when(both)


def position():
    section = lax.axis_index("section")
    odd = lax.rem(section, 2) == 1
    return (
        odd,
        jnp.logical_not(odd),
        section == 0,
        section == lax.axis_size("section") - 1,
    )


class Halves:
    def __init__(self, copies):
        self.copies = copies

    def start(self):
        for copy in self.copies:
            copy.start()

    def wait(self):
        for copy in self.copies:
            copy.wait()


def split(source, targets, sems, first, second):
    half = source.shape[0] // 2
    return Halves(
        [
            pltpu.make_async_copy(source.at[pl.ds(i * half, half)], targets[i], sems.at[k])
            for i, k in enumerate((first, second))
        ]
    )


def join(sources, target, sems, first, second):
    half = target.shape[0] // 2
    return Halves(
        [
            pltpu.make_async_copy(sources[i], target.at[pl.ds(i * half, half)], sems.at[k])
            for i, k in enumerate((first, second))
        ]
    )


class Across:
    def __init__(self, parts, target, sems, first, second):
        low, high, relayed = parts
        self.plain = join((low, high), target, sems, first, second)
        self.middle = join((low, relayed), target, sems, first, second)
        section = lax.axis_index("section")
        half = lax.axis_size("section") // 2
        self.inside = jnp.logical_or(section == half - 1, section == half)

    def start(self):
        pl.when(self.inside)(self.middle.start)
        pl.when(jnp.logical_not(self.inside))(self.plain.start)

    def wait(self):
        pl.when(self.inside)(self.middle.wait)
        pl.when(jnp.logical_not(self.inside))(self.plain.wait)


def fetch(cases, x_s, b_s, r_s, sems):
    moves = []
    for predicates, source, routes in cases:
        narrow = not isinstance(source, Across) and source.dtype == BF16
        mine = [source]
        if not isinstance(source, Across):
            mine = [pltpu.make_async_copy(source, b_s if narrow else x_s, sems.at[0])]
        if routes is not None:
            mine.append(pltpu.make_async_copy(routes, r_s, sems.at[1]))
        moves.append((predicates, narrow, mine))

        @when_all(*predicates)
        def _(mine=mine):
            for copy in mine:
                copy.start()

    def wait():
        for predicates, narrow, mine in moves:

            @when_all(*predicates)
            def _(narrow=narrow, mine=mine):
                for copy in mine:
                    copy.wait()
                if narrow:
                    x_s[...] = b_s[...].astype(F32)

    return wait


NAMES = ("gain", "router", "a", "gate", "up", "b", "down")


def fetch_weights(hbm, weights, order, sems):
    copies = {}
    for name in order:
        i = NAMES.index(name)
        copies[name] = pltpu.make_async_copy(hbm[i], weights[i], sems.at[i])
        copies[name].start()
    return copies


def primal_of(x, routes, copies, weights):
    gain_s, router, a_t, gate, up, factors = weights[:6]
    if copies is not None:
        copies["gain"].wait()
    return primal(x, routes, gain_s[...], copies, router, a_t, gate, up, factors)


def output_of(x_s, values, down):
    _, _, _, weight, _, gate_pre, up_pre = values
    hidden = (gate_pre * jax.nn.sigmoid(gate_pre) * up_pre).astype(BF16)
    return x_s[...] + weight * nn(hidden, down[...])


def gradients(x_s, g_s, saved, weights, copies=None, late=None):
    def ready(*names):
        if copies is not None:
            for name in names:
                copies[name].wait()

    gain_s, router, a_t, gate, up, factors, down = weights
    if late is None:
        rstd, normed, share, weight, low, gate_pre, up_pre = saved
    else:
        share, gate_pre, up_pre = (saved[i][...] for i in (2, 4, 5))
        weight = share[:, 0:1]
    sig = jax.nn.sigmoid(gate_pre)
    silu = gate_pre * sig
    hidden = (silu * up_pre).astype(BF16)
    ready("down")
    back = nt(g_s[...].astype(BF16), down[...])
    d_weight = jnp.sum(hidden.astype(F32) * back, axis=-1, keepdims=True)
    lead = (lax.broadcasted_iota(jnp.int32, share.shape, 1) == 0).astype(F32)
    d_logits = ((d_weight * weight) * (lead - share)).astype(BF16)
    d_hidden = (weight * back).astype(BF16).astype(F32)
    d_gate = (d_hidden * up_pre * (sig * (1.0 + gate_pre * (1.0 - sig)))).astype(BF16)
    d_up = (d_hidden * silu).astype(BF16)
    ready("b", "gate", "up", "router", "a", "gain")
    if late is not None:
        rstd, normed, low = late()
    d_low_f = SCALE * jnp.concatenate([nt(d_gate, factors[0]), nt(d_up, factors[1])], axis=1)
    d_normed = (
        nt(d_gate, gate[...])
        + nt(d_up, up[...])
        + nt(d_logits, router[...])
        + nn(d_low_f.astype(BF16), a_t[...])
    )
    scaled = d_normed * gain_s[...]
    x = x_s[...]
    along = jnp.mean(scaled * x, axis=-1, keepdims=True) * (rstd * rstd)
    dx = g_s[...] + rstd * (scaled - x * along)
    rank = low.shape[1] // 2
    ga = nn(d_low_f.T.astype(BF16), normed)
    low_t = low.astype(F32).T.astype(BF16)
    gb = SCALE * jnp.concatenate([nn(low_t[:rank], d_gate), nn(low_t[rank:], d_up)], axis=0)
    return dx, ga, gb


def normalizer(ga, gb, mean_scale):
    square = (jnp.sum(ga * ga) + jnp.sum(gb * gb)) / (ga.size + gb.size)
    return lax.rsqrt(square + EPS) * mean_scale


def pack(packed, ga, gb):
    gb_t = gb.T
    ys, _, width = packed.shape
    zs = ga.shape[1] // (ys * width)
    size = packed.shape[1] // zs
    rows = gb_t.shape[0] // (ys * zs)
    tall = ga.shape[0]
    half = rows // 2
    for y in range(ys):
        for z in range(zs):
            p = z * ys + y
            at = z * size
            packed[y, at : at + tall, :] = ga[:, p * width : (p + 1) * width]
            at += tall
            packed[y, at : at + half, :tall] = gb_t[p * rows : p * rows + half]
            packed[y, at : at + half, tall:] = gb_t[p * rows + half : (p + 1) * rows]
            packed[y, at + half : (z + 1) * size, :] = jnp.zeros((size - tall - half, width), F32)


FIRST_ORDER = ("gain", "router", "a", "b", "gate", "up", "down")
X1, X2, G, W, OUT = (pl.ds(0, 2), pl.ds(2, 2), pl.ds(4, 2), pl.ds(6, 7), pl.ds(13, 7))


def first_kernel(
    mean_scale, plan, arriving, returning, examples, stash, fwd_routes_t, bwd_routes_t, *rest
):
    hbm, (*slow_o, fast_o, ga_o, gb_o), rest = rest[:7], rest[7:12], rest[12:]
    x_s, x2_s, g_s, y_s, d_s, b_s, b2_s, e_s, r_s, r2_s, ga_s, gb_s, *weights, sems = rest
    odd, even, first, last = position()
    slot = plan[0, 0]
    mine = fwd_routes_t.at[0]
    x_wait = fetch(
        [
            ((first,), examples.at[0], mine),
            ((jnp.logical_not(first),), arriving, mine),
        ],
        x_s,
        b_s,
        r_s,
        sems.at[X1],
    )
    copies = fetch_weights(hbm, weights, FIRST_ORDER, sems.at[W])
    x2_wait = fetch(
        [
            ((last,), arriving, mine),
            ((jnp.logical_not(last),), stash.at[slot], bwd_routes_t.at[slot]),
        ],
        x2_s,
        b2_s,
        r2_s,
        sems.at[X2],
    )
    g_copy = pltpu.make_async_copy(returning, g_s, sems.at[4])
    t_copy = pltpu.make_async_copy(examples.at[0], e_s, sems.at[5])
    pl.when(jnp.logical_not(last))(g_copy.start)
    pl.when(last)(t_copy.start)
    x_wait()
    values = primal_of(x_s[...], r_s[...], copies, weights)
    copies["down"].wait()
    y_s[...] = output_of(x_s, values, weights[6])
    outs = sems.at[OUT]
    y_slow = split(y_s, slow_o, outs, 0, 4)
    y_fast = pltpu.make_async_copy(y_s, fast_o, outs.at[0])
    d_slow = split(d_s, slow_o, outs, 1, 5)
    d_fast = pltpu.make_async_copy(d_s, fast_o, outs.at[1])
    pl.when(odd)(y_slow.start)
    pl.when(even)(y_fast.start)
    x2_wait()

    @pl.when(last)
    def _():
        t_copy.wait()
        g_s[...] = y_s[...] - e_s[...].astype(F32)

    values = primal_of(x2_s[...], r2_s[...], None, weights)
    pl.when(jnp.logical_not(last))(g_copy.wait)
    dx, ga, gb = gradients(x2_s, g_s, values, weights)
    d_s[...] = dx
    pl.when(odd)(d_fast.start)
    pl.when(even)(d_slow.start)
    factor = normalizer(ga, gb, mean_scale)
    ga_s[...] = factor * ga
    gb_s[...] = factor * gb
    tail = [
        pltpu.make_async_copy(ga_s, ga_o, outs.at[2]),
        pltpu.make_async_copy(gb_s, gb_o, outs.at[3]),
    ]
    for copy in tail:
        copy.start()
    for copy in tail:
        copy.wait()

    @pl.when(odd)
    def _():
        y_slow.wait()
        d_fast.wait()

    @pl.when(even)
    def _():
        y_fast.wait()
        d_slow.wait()


def fill_kernel(gain, token, gain_s, sem):
    copy = pltpu.make_async_copy(gain, gain_s, sem)
    copy.start()
    copy.wait()
    token[...] = jnp.broadcast_to(gain_s[:, :128], token.shape)


def second_kernel(
    tick, mean_scale, plan, arrived, after, stash, fwd_routes_t, bwd_routes_t, ga_in, gb_in, *rest
):
    hbm, (*sent, packed), saved_o, rest = rest[:7], rest[7:10], rest[10:16], rest[16:]
    x_s, x2_s, y_s, b_s, b2_s, r_s, r2_s, ga_s, gb_s, packed_s, *rest = rest
    saved, weights, sems = rest[:6], rest[6:13], rest[13]
    odd, even, _, last = position()
    slot = plan[0, tick]
    mine = fwd_routes_t.at[tick]
    stored = (stash.at[slot], bwd_routes_t.at[slot])
    inner = jnp.logical_and(odd, jnp.logical_not(last))
    x_wait = fetch([((odd,), arrived, mine), ((even,), *stored)], x_s, b_s, r_s, sems.at[X1])
    copies = fetch_weights(hbm, weights, FIRST_ORDER, sems.at[W])
    x2_wait = fetch(
        [((last,), arrived, mine), ((inner,), *stored)], x2_s, b2_s, r2_s, sems.at[X2]
    )
    g_copies = [
        pltpu.make_async_copy(arrived, x2_s, sems.at[4]),
        pltpu.make_async_copy(ga_in, ga_s, sems.at[5]),
        pltpu.make_async_copy(gb_in, gb_s, sems.at[20]),
    ]

    @pl.when(even)
    def _():
        for copy in g_copies:
            copy.start()

    x_wait()
    values = primal_of(x_s[...], r_s[...], copies, weights)
    copies["down"].wait()
    outs = sems.at[OUT]
    y_copy = split(y_s, sent, sems, 13, 21)

    @pl.when(odd)
    def _():
        y_s[...] = output_of(x_s, values, weights[6])
        y_copy.start()
        x2_wait()
        rstd, normed, share, _, low, gate_pre, up_pre = primal_of(
            x2_s[...], r2_s[...], None, weights
        )
        kept = (jnp.broadcast_to(rstd, saved[0].shape), normed, share, low, gate_pre, up_pre)
        moves = []
        for i, value in enumerate(kept):
            saved[i][...] = value
            moves.append(pltpu.make_async_copy(saved[i], saved_o[i], outs.at[1 + i]))
            moves[-1].start()
        for move in moves:
            move.wait()

    @pl.when(even)
    def _():
        for copy in g_copies:
            copy.wait()
        dx, ga, gb = gradients(x_s, x2_s, values, weights)
        y_s[...] = dx
        y_copy.start()
        factor = normalizer(ga, gb, mean_scale)
        pack(packed_s, ga_s[...] + factor * ga, gb_s[...] + factor * gb)
        move = pltpu.make_async_copy(packed_s, packed, outs.at[1])
        move.start()
        move.wait()

    y_copy.wait()


def third_kernel(
    tick,
    mean_scale,
    plan,
    low,
    high,
    relayed,
    near,
    output_low,
    output_high,
    examples,
    stash,
    fwd_routes_t,
    packed_in,
    ga_in,
    gb_in,
    *rest,
):
    saved_in, rest = rest[:6], rest[6:]
    hbm, (sent, packed), rest = rest[:7], rest[7:9], rest[9:]
    x_s, g_s, y_s, b_s, e_s, r_s, ga_s, gb_s, packed_s, *rest = rest
    saved, weights, sems = rest[:6], rest[6:13], rest[13]
    odd, even, first, last = position()
    inner = jnp.logical_and(odd, jnp.logical_not(last))
    outs = sems.at[OUT]
    parts = (low, high, relayed)
    y_copy = pltpu.make_async_copy(y_s, sent, outs.at[0])
    p_copy = pltpu.make_async_copy(packed_s, packed, sems.at[20])

    @pl.when(even)
    def _():
        mine = fwd_routes_t.at[tick]
        x_wait = fetch(
            [
                ((first,), examples.at[tick], mine),
                ((jnp.logical_not(first),), Across(parts, x_s, sems, 0, 21), mine),
            ],
            x_s,
            b_s,
            r_s,
            sems.at[X1],
        )
        copies = fetch_weights(hbm, weights, FIRST_ORDER, sems.at[W])
        keep = pltpu.make_async_copy(packed_in, packed_s, sems.at[4])
        keep.start()
        x_wait()
        values = primal_of(x_s[...], r_s[...], copies, weights)
        copies["down"].wait()
        keep.wait()
        p_copy.start()
        y_s[...] = output_of(x_s, values, weights[6])
        y_copy.start()

    @pl.when(odd)
    def _():
        g_copy = Across(parts, g_s, sems, 4, 21)
        o_copy = join((output_low, output_high), g_s, sems, 4, 21)
        t_copy = pltpu.make_async_copy(examples.at[tick], e_s, sems.at[5])
        pl.when(inner)(g_copy.start)

        @pl.when(last)
        def _():
            o_copy.start()
            t_copy.start()

        moves = [pltpu.make_async_copy(saved_in[i], saved[i], outs.at[1 + i]) for i in range(6)]
        for i in (2, 4, 5):
            moves[i].start()
        copies = fetch_weights(hbm, weights, ("down", "gate", "up", "b", "router", "a"), sems.at[W])
        for i in (0, 1, 3):
            moves[i].start()
        x_wait = fetch(
            [((last,), near, None), ((inner,), stash.at[plan[0, tick]], None)],
            x_s,
            b_s,
            None,
            sems.at[X1],
        )
        copies.update(fetch_weights(hbm, weights, ("gain",), sems.at[W]))
        sums = [
            pltpu.make_async_copy(ga_in, ga_s, sems.at[2]),
            pltpu.make_async_copy(gb_in, gb_s, sems.at[3]),
        ]
        for copy in sums:
            copy.start()
        for i in (2, 4, 5):
            moves[i].wait()
        pl.when(inner)(g_copy.wait)

        @pl.when(last)
        def _():
            o_copy.wait()
            t_copy.wait()
            g_s[...] = g_s[...] - e_s[...].astype(F32)

        def late():
            for i in (0, 1, 3):
                moves[i].wait()
            x_wait()
            return saved[0][:, 0:1], saved[1][...], saved[3][...]

        dx, ga, gb = gradients(x_s, g_s, saved, weights, copies, late)
        y_s[...] = dx
        y_copy.start()
        factor = normalizer(ga, gb, mean_scale)
        for copy in sums:
            copy.wait()
        pack(packed_s, ga_s[...] + factor * ga, gb_s[...] + factor * gb)
        p_copy.start()

    y_copy.wait()
    p_copy.wait()


def sum_kernel(parts, total):
    total[...] = jnp.sum(parts[...], axis=0).reshape(total.shape)


class Choice:
    def __init__(self, refs, rows, target, sem):
        self.copies = [pltpu.make_async_copy(ref.at[rows], target, sem) for ref in refs]
        section = lax.axis_index("section")
        count = lax.axis_size("section")
        middle = jnp.logical_or(section == count // 2 - 1, section == count // 2)
        ends = jnp.logical_or(section == 0, section == count - 1)
        self.inside = jnp.logical_or(middle, ends)

    def start(self):
        pl.when(self.inside)(self.copies[1].start)
        pl.when(jnp.logical_not(self.inside))(self.copies[0].start)

    def wait(self):
        pl.when(self.inside)(self.copies[1].wait)
        pl.when(jnp.logical_not(self.inside))(self.copies[0].wait)


def final_kernel(tall, half, pieces, parts, low, high, relayed, fast, ga, gb, acts_o, grads_o, slow_s, fast_s, sems):
    odd, even, _, _ = position()
    rows = fast.shape[0] // pieces
    moves = []
    for source, stage, even_o, odd_o in (
        (None, slow_s, acts_o, grads_o),
        (fast, fast_s, grads_o, acts_o),
    ):
        for i in range(pieces):
            at = pl.ds(i * rows, rows)
            k = 2 * len(moves)
            if source is None:
                within = pl.ds((i % (pieces // 2)) * rows, rows)
                refs = (low, low) if i < pieces // 2 else (high, relayed)
                move_in = Choice(refs, within, stage.at[at], sems.at[k])
            else:
                move_in = pltpu.make_async_copy(source.at[at], stage.at[at], sems.at[k])
            move_even = pltpu.make_async_copy(stage.at[at], even_o.at[at], sems.at[k + 1])
            move_odd = pltpu.make_async_copy(stage.at[at], odd_o.at[at], sems.at[k + 1])
            moves.append((move_in, move_even, move_odd))
    for move_in, _, _ in moves:
        move_in.start()
    for move_in, move_even, move_odd in moves:
        move_in.wait()
        pl.when(even)(move_even.start)
        pl.when(odd)(move_odd.start)
    total = jnp.sum(parts[...], axis=0)
    ga[...] = total[:tall]
    rank = gb.shape[2]
    for side in range(2):
        for part in range(2):
            lane = part * tall + side * rank
            gb[side, part * half : (part + 1) * half, :] = total[
                tall : tall + half, lane : lane + rank
            ]
    for _, move_even, move_odd in moves:
        pl.when(even)(move_even.wait)
        pl.when(odd)(move_odd.wait)


def swaps(first, count):
    pairs = []
    for s in range(first, count - 1, 2):
        pairs += [(s, s + 1), (s + 1, s)]
    return pairs


def shards(
    y_size,
    examples,
    arriving,
    returning,
    stash,
    plan,
    forward_expert_routes,
    backward_expert_routes,
    input_norm_gain,
    router,
    frozen_gate_weight,
    frozen_up_weight,
    frozen_down_weight,
    down_factors,
    up_factors,
):
    replicas = lax.axis_size("dp")
    z_size = replicas // y_size
    ticks, tokens, width = examples.shape
    mean_scale = 1.0 / (ticks * replicas)
    gain, router, gate, up, down = (
        input_norm_gain,
        router[0],
        frozen_gate_weight[0],
        frozen_up_weight[0],
        frozen_down_weight[0],
    )
    a_t = down_factors[0].T
    b = up_factors[0]
    stash = stash[0]
    fwd_routes_t = jnp.swapaxes(forward_expert_routes[0], 1, 2)
    bwd_routes_t = jnp.swapaxes(backward_expert_routes[0], 1, 2)
    topk = fwd_routes_t.shape[1]
    hidden_units = gate.shape[1]
    columns = a_t.shape[0]
    weights = (gain, router, a_t, gate, up, b, down)
    scratch = [pltpu.VMEM(w.shape, w.dtype) for w in weights]
    x_scratch = pltpu.VMEM((tokens, width), F32)
    b_scratch = pltpu.VMEM((tokens, width), BF16)
    r_scratch = pltpu.VMEM((topk, tokens), jnp.int32)
    semaphores = pltpu.SemaphoreType.DMA((22,))
    sections = lax.axis_size("section")
    near = swaps(0, sections)
    far = swaps(1, sections)
    mid = sections // 2 - 1
    around = [p for p in far if p not in ((mid, mid + 1), (mid + 1, mid))]
    around += [(mid, 0), (mid + 1, sections - 1)]
    relays = [(0, mid + 1), (sections - 1, mid)]

    def far_swap(low, high):
        high = lax.ppermute(high, "section", around)
        low = lax.ppermute(low, "section", far)
        relayed = lax.ppermute(high, "section", relays)
        return low, high, relayed

    rows_each = hidden_units // replicas
    size = columns + -(-(rows_each // 2) // 8) * 8
    share_width = width // replicas
    activation = jax.ShapeDtypeStruct((tokens, width), F32)
    half_activation = jax.ShapeDtypeStruct((tokens // 2, width), F32)
    sums_shape = (
        jax.ShapeDtypeStruct((columns, width), F32),
        jax.ShapeDtypeStruct((columns, hidden_units), F32),
    )
    packed_shape = jax.ShapeDtypeStruct((y_size, z_size * size, share_width), F32)
    saved_shape = (
        jax.ShapeDtypeStruct((tokens, 128), F32),
        jax.ShapeDtypeStruct((tokens, width), BF16),
        jax.ShapeDtypeStruct((tokens, router.shape[1]), F32),
        jax.ShapeDtypeStruct((tokens, columns), BF16),
        jax.ShapeDtypeStruct((tokens, hidden_units), F32),
        jax.ShapeDtypeStruct((tokens, hidden_units), F32),
    )

    def rooms(shapes):
        return [pltpu.VMEM(shape.shape, shape.dtype) for shape in shapes]

    primal_flops = 2 * tokens * width * (router.shape[1] + columns + 2 * hidden_units)
    down_flops = 2 * tokens * width * hidden_units
    weight_bytes = sum(w.size * w.dtype.itemsize for w in weights)

    def kernel(body, flops, outs, rooms, operands):
        return pl.pallas_call(
            body,
            out_shape=outs,
            in_specs=[SMEM] + [ANY] * (len(operands) - 1),
            out_specs=(ANY,) * len(outs),
            scratch_shapes=[*rooms, *scratch, semaphores],
            compiler_params=pltpu.CompilerParams(vmem_limit_bytes=67043328),
            cost_estimate=pl.CostEstimate(
                flops=flops, bytes_accessed=weight_bytes + 8 * tokens * width, transcendentals=0
            ),
        )(*operands)

    low, high, fast, *sums = kernel(
        functools.partial(first_kernel, mean_scale),
        3 * primal_flops + 2 * down_flops,
        (half_activation, half_activation, activation, *sums_shape),
        [x_scratch] * 5 + [b_scratch] * 3 + [r_scratch] * 2 + rooms(sums_shape),
        (plan, arriving[0], returning[0], examples, stash, fwd_routes_t, bwd_routes_t, *weights),
    )
    slow_0 = far_swap(low, high)
    fast_0 = lax.ppermute(fast, "section", near)
    whole = pltpu.CompilerParams(vmem_limit_bytes=67043328)
    token = pl.pallas_call(
        fill_kernel,
        out_shape=jax.ShapeDtypeStruct((8, 128), F32),
        in_specs=[ANY],
        out_specs=VMEM,
        scratch_shapes=[pltpu.VMEM(gain.shape, F32), pltpu.SemaphoreType.DMA],
        compiler_params=whole,
        name="fill",
    )(gain)
    *ahead, packed, s0, s1, s2, s3, s4, s5 = kernel(
        functools.partial(second_kernel, 1, mean_scale),
        2 * primal_flops + down_flops,
        (half_activation, half_activation, packed_shape, *saved_shape),
        [x_scratch] * 3
        + [b_scratch] * 2
        + [r_scratch] * 2
        + rooms((*sums_shape, packed_shape, *saved_shape)),
        (plan, fast_0, token, stash, fwd_routes_t, bwd_routes_t, *sums, *weights),
    )
    saved = (s0, s1, s2, s3, s4, s5)
    slow_1 = far_swap(*ahead)
    sent, packed = kernel(
        functools.partial(third_kernel, 1, mean_scale),
        primal_flops + down_flops,
        (activation, packed_shape),
        [x_scratch] * 3
        + [b_scratch] * 2
        + [r_scratch]
        + rooms((*sums_shape, packed_shape, *saved_shape)),
        (plan, *slow_0, fast_0, *ahead, examples, stash, fwd_routes_t, packed, *sums, *saved, *weights),
    )
    y_groups = [[z * y_size + y for y in range(y_size)] for z in range(z_size)]
    z_groups = [[z * y_size + y for z in range(z_size)] for y in range(y_size)]
    parts = lax.all_to_all(packed, "dp", 0, 0, axis_index_groups=y_groups, tiled=True)
    fast_1 = lax.ppermute(sent, "section", near)
    parts = pl.pallas_call(
        sum_kernel,
        out_shape=jax.ShapeDtypeStruct((z_size, size, share_width), F32),
        in_specs=[VMEM],
        out_specs=VMEM,
        compiler_params=pltpu.CompilerParams(vmem_limit_bytes=8 << 20),
        name="sum_y",
    )(parts)
    parts, slow_1 = lax.optimization_barrier((parts, slow_1))
    parts = lax.all_to_all(parts, "dp", 0, 0, axis_index_groups=z_groups, tiled=True)
    pieces = 4
    share_a, share_b, next_acts, next_grads = pl.pallas_call(
        functools.partial(final_kernel, columns, rows_each // 2, pieces),
        out_shape=(
            jax.ShapeDtypeStruct((columns, share_width), F32),
            jax.ShapeDtypeStruct((2, rows_each, columns // 2), F32),
            activation,
            activation,
        ),
        in_specs=[VMEM, ANY, ANY, ANY, ANY],
        out_specs=(VMEM, VMEM, ANY, ANY),
        scratch_shapes=[x_scratch, x_scratch, pltpu.SemaphoreType.DMA((4 * pieces,))],
        compiler_params=pltpu.CompilerParams(vmem_limit_bytes=8 << 20),
        name="sum_dp",
    )(parts, *slow_1, fast_1)
    return (
        next_acts[None],
        next_grads[None],
        share_a.T[None],
        jnp.swapaxes(share_b, 1, 2)[None],
    )


def solution(mesh):
    in_specs = (
        P(None, "dp", None),
        P("section", "dp", None),
        P("section", "dp", None),
        P("section", None, "dp", None),
        P("section", None),
        P("section", None, "dp", None),
        P("section", None, "dp", None),
        P("section", None),
        P("section", None, None),
        P("section", None, None),
        P("section", None, None),
        P("section", None, None),
        P("section", None, None),
        P("section", None, None, None),
    )
    out_specs = (
        P("section", "dp", None),
        P("section", "dp", None),
        P("section", "dp", None),
        P("section", None, None, "dp"),
    )

    def body(*args):
        return shards(4, *args)

    return jax.shard_map(
        body, mesh=mesh, in_specs=in_specs, out_specs=out_specs, check_vma=False
    )
```
